512 devices in a mesh: lon: 128 (over y, x_hi, z), lat: 4 (over x_lo, core).
Axes of the slice: x: 4 (x_hi: 2, x_lo: 2; x = x_hi * 2 + x_lo), y: 8, z: 8, core: 2. Of those that a mesh axis runs over, the one named last changes fastest.
Arguments:
- obs_rows: bfloat16 [128, 4, 1024, 64], P('lon', 'lat'), may hold values from -6 to 6
- obs_cells: int32 [128, 4, 1024], P('lon', 'lat'), may hold values from 0 to 63
- obs_counts: int32 [128, 4], P('lon', 'lat'), may hold values from 128 to 1024, as said below
- enc_weight: bfloat16 [64, 1024], replicated, may hold values from -0.75 to 0.75
- near_kernel_weight: bfloat16 [3, 3, 64, 1024], replicated, may hold values from -0.25 to 0.25
- far_kernel_weight: bfloat16 [3, 3, 64, 1024], replicated, may hold values from -0.25 to 0.25
- mix_weight: bfloat16 [1024, 1024], replicated, may hold values from -0.1875 to 0.1875
Outputs:
- state: bfloat16 [1024, 32, 1024], P('lon', 'lat')
The draws below stay inside these ranges and needn't reach their ends.
Inputs may be any that keep to these rules, and one draw needn't show every extreme that they name: `obs_cells`: cell index i * 8 + j within the sector and band; slots at or past the count are ignored. `obs_counts`: live slots come first; some sector and band has all 1024 slots live.
All inputs are finite; a program needn't handle non-finite values.
Results may differ from the reference program's by a relative error of at most 0.006.
Values may be sent and summed in bfloat16 or wider, within the bound.
A program may use at most 128 MiB of HBM per device.

```python
import jax
import jax.numpy as jnp
from jax import lax

C = 1024
F_OBS = 64
FAR_DILATION = 8
BAND_LAT_CELLS = 8
R_CAP = 1024
SECTOR_LON_CELLS = 8
GW = 64
SECTORS = 128
BANDS = 4
NLON = 1024
GRID_LAT_CELLS = 32


def draw_obs_counts(key, part):
    first_key = jax.random.fold_in(key, 11)
    second_key = jax.random.fold_in(key, 23)
    levels = jax.random.randint(first_key, (SECTORS, BANDS), 0, 4)
    counts = R_CAP // jnp.left_shift(jnp.ones_like(levels), levels)
    chosen = jax.random.randint(second_key, (), 0, SECTORS * BANDS)
    flat_index = jnp.arange(SECTORS * BANDS).reshape(SECTORS, BANDS)
    return jnp.where(flat_index == chosen, R_CAP, counts).astype(jnp.int32)


def with_ends(array, own_key, least, high):
    dims = array.shape
    spot = [jax.random.randint(jax.random.fold_in(own_key, axis), (), 0, dims[axis]) for axis in range(len(dims))]
    array = array.at[tuple(spot)].set(least)
    longest = dims.index(max(dims))
    spot[longest] = (spot[longest] + 1) % dims[longest]
    return array.at[tuple(spot)].set(high)


def block_levels(own_key, dims, shards, low, high):
    factor_of = 1.0
    for position, parts in shards:
        heights = jax.random.uniform(jax.random.fold_in(jax.random.fold_in(own_key, 6), position), (parts,), jnp.float32, low / len(shards), high / len(shards))
        factor_of = factor_of * jnp.repeat(jnp.exp(heights), dims[position] // parts).reshape((-1,) + (1,) * (len(dims) - 1 - position))
    return factor_of


def normal_values(stream_key, dims, scale, reach, cuts=(), kind=jnp.bfloat16):
    drawn = jax.random.normal(stream_key, dims, jnp.float32) * scale
    if len(cuts) > 0:
        drawn = block_levels(stream_key, dims, cuts, -0.22, 0.18) * drawn
    return jnp.clip(drawn, min=-reach, max=reach).astype(kind)


def setup_inputs(seed: int = 0) -> dict:
    keys = jax.random.split(jax.random.key(seed), 8)
    obs_rows = normal_values(keys[0], (SECTORS, BANDS, R_CAP, F_OBS), 1.0, 6.0, ((0, 128), (1, 4)))
    obs_cells = with_ends(jax.random.randint(keys[1], (SECTORS, BANDS, R_CAP), 0, SECTOR_LON_CELLS * BAND_LAT_CELLS), jax.random.fold_in(keys[1], 1), 0, (SECTOR_LON_CELLS * BAND_LAT_CELLS) - 1).astype(jnp.int32)
    obs_counts = draw_obs_counts(jax.random.fold_in(keys[7], 71), 0)
    enc_weight = normal_values(keys[3], (F_OBS, C), F_OBS ** -0.5, 0.75)
    near_kernel_weight = normal_values(keys[4], (3, 3, GW, C), (9 * GW) ** -0.5, 0.25)
    far_kernel_weight = normal_values(keys[5], (3, 3, GW, C), (9 * GW) ** -0.5, 0.25)
    mix_weight = normal_values(keys[6], (C, C), C ** -0.5, 0.1875)
    return {"obs_rows": obs_rows, "obs_cells": obs_cells, "obs_counts": obs_counts, "enc_weight": enc_weight, "near_kernel_weight": near_kernel_weight, "far_kernel_weight": far_kernel_weight, "mix_weight": mix_weight}


def grouped_filter(extended, lon_starts, lat_starts, rows, cols, weight):
    pieces = [extended[p:p + rows, q:q + cols] for p in lon_starts for q in lat_starts]
    stacked = jnp.stack(pieces, 0).astype(jnp.float32)
    channels = stacked.shape[-1]
    width = weight.shape[2]
    groups = channels // width
    taps = stacked.reshape(9, rows * cols, groups, width)
    kernel = weight.astype(jnp.float32).reshape(9, width, groups, width)
    return jnp.einsum('tngi,tigo->ngo', taps, kernel).reshape(rows, cols, channels)


def reference(obs_rows, obs_cells, obs_counts, enc_weight, near_kernel_weight, far_kernel_weight, mix_weight):
    slots = jnp.arange(R_CAP, dtype=jnp.int32)
    band_index = jnp.arange(BANDS, dtype=jnp.int32)[:, None]

    def encode_sector(sector):
        sector_rows = lax.dynamic_index_in_dim(obs_rows, sector, 0, keepdims=False)
        sector_cells = lax.dynamic_index_in_dim(obs_cells, sector, 0, keepdims=False)
        sector_counts = lax.dynamic_index_in_dim(obs_counts, sector, 0, keepdims=False)
        encoded = jnp.dot(sector_rows.reshape(BANDS * R_CAP, F_OBS), enc_weight,
                          preferred_element_type=jnp.float32).astype(jnp.bfloat16)
        live_slot = (slots[None, :] < sector_counts[:, None]).reshape(-1, 1)
        placed = (sector_cells // BAND_LAT_CELLS) * GRID_LAT_CELLS + band_index * BAND_LAT_CELLS + sector_cells % BAND_LAT_CELLS
        values = jnp.where(live_slot, encoded.astype(jnp.float32), jnp.zeros((), jnp.float32))
        summed = jax.ops.segment_sum(values, placed.reshape(-1).astype(jnp.int32), num_segments=SECTOR_LON_CELLS * GRID_LAT_CELLS)
        return summed.astype(jnp.bfloat16).reshape(SECTOR_LON_CELLS, GRID_LAT_CELLS, C)

    input_field = lax.map(encode_sector, jnp.arange(SECTORS, dtype=jnp.int32)).reshape(NLON, GRID_LAT_CELLS, C)
    wrapped_field = jnp.concatenate([input_field[NLON - SECTOR_LON_CELLS:], input_field, input_field[:SECTOR_LON_CELLS]], 0)
    padded_field = jnp.pad(wrapped_field, ((0, 0), (FAR_DILATION, FAR_DILATION), (0, 0)))

    def sector_out(sector):
        block_tile = lax.dynamic_slice_in_dim(padded_field, sector * SECTOR_LON_CELLS, 3 * SECTOR_LON_CELLS, 0)
        centre_cells = block_tile[SECTOR_LON_CELLS:2 * SECTOR_LON_CELLS, FAR_DILATION:FAR_DILATION + GRID_LAT_CELLS].astype(jnp.float32)
        near_output = grouped_filter(block_tile, [SECTOR_LON_CELLS - 1, SECTOR_LON_CELLS, SECTOR_LON_CELLS + 1], [FAR_DILATION - 1, FAR_DILATION, FAR_DILATION + 1], SECTOR_LON_CELLS, GRID_LAT_CELLS, near_kernel_weight)
        far_output = grouped_filter(block_tile, [0, SECTOR_LON_CELLS, 2 * SECTOR_LON_CELLS], [0, FAR_DILATION, 2 * FAR_DILATION], SECTOR_LON_CELLS, GRID_LAT_CELLS, far_kernel_weight)
        total = centre_cells + near_output + far_output
        activ = jax.nn.gelu(total, approximate=True).astype(jnp.bfloat16)
        mixed = jnp.dot(activ.reshape(SECTOR_LON_CELLS * GRID_LAT_CELLS, C), mix_weight,
                        preferred_element_type=jnp.float32).reshape(SECTOR_LON_CELLS, GRID_LAT_CELLS, C)
        return (total + mixed).astype(jnp.bfloat16)

    return lax.map(sector_out, jnp.arange(SECTORS, dtype=jnp.int32)).reshape(NLON, GRID_LAT_CELLS, C)
```

```python
import functools

import jax
import jax.numpy as jnp
from jax import lax
from jax.experimental import pallas as pl
from jax.experimental.pallas import tpu as pltpu
from jax.sharding import PartitionSpec as P

LON = 8
LAT = 8
CELLS = LON * LAT
MESH = pl.DeviceIdType.MESH
OFFSETS = [(a, b) for a in (-1, 0, 1) for b in (-1, 0, 1)]
CENTRE = 4
CHUNK = 256


def slot_of(a, b):
    return (a + 1) * 3 + (b + 1)


def composite(enc, weight_ref, composite_ref, base, low_mask, high_mask):
    features, channels = enc.shape
    zero = jnp.zeros((features, 128), jnp.bfloat16)

    def tap(t, carry):
        taps = weight_ref[t // 3, t % 3]
        for start in range(0, channels, CHUNK):
            left = taps[:, start : start + 128]
            right = taps[:, start + 128 : start + 256]
            blocks = jnp.concatenate(
                [
                    jnp.concatenate([left * low_mask, zero], axis=1),
                    jnp.concatenate([left * high_mask, zero], axis=1),
                    jnp.concatenate([zero, right * low_mask], axis=1),
                    jnp.concatenate([zero, right * high_mask], axis=1),
                ],
                axis=0,
            )
            product = jnp.dot(
                enc[:, start : start + CHUNK], blocks, preferred_element_type=jnp.float32
            )
            row = pl.multiple_of((base + t) * features, features)
            composite_ref[pl.ds(row, features), start : start + CHUNK] = product.astype(
                jnp.bfloat16
            )
        return carry

    lax.fori_loop(0, 9, tap, 0)


def kernel(
    lon_count,
    lat_count,
    obs_hbm,
    cells_hbm,
    count_hbm,
    enc_hbm,
    near_hbm,
    far_hbm,
    mix_hbm,
    out_ref,
    obs_ref,
    cells_ref,
    count_ref,
    enc_ref,
    near_ref,
    far_ref,
    mix_ref,
    slots,
    composite_ref,
    total_ref,
    activ_ref,
    local_sems,
    send_sems,
    recv_sems,
):
    pairs = [
        (obs_hbm, obs_ref),
        (cells_hbm, cells_ref),
        (count_hbm, count_ref),
        (enc_hbm, enc_ref),
        (near_hbm, near_ref),
        (far_hbm, far_ref),
        (mix_hbm, mix_ref),
    ]
    loads = [
        pltpu.make_async_copy(source, target, local_sems.at[i])
        for i, (source, target) in enumerate(pairs)
    ]
    for load in loads:
        load.start()

    lon = lax.axis_index("lon")
    lat = lax.axis_index("lat")

    def peer(a, b):
        return {"lon": lax.rem(lon + a + lon_count, lon_count), "lat": lat + b}

    def with_peer(b, body):
        if b == 0:
            body()
        elif b < 0:
            pl.when(lat > 0)(body)
        else:
            pl.when(lat < lat_count - 1)(body)

    remote = [(a, b) for a, b in OFFSETS if (a, b) != (0, 0)]
    barrier = pltpu.get_barrier_semaphore()
    for a, b in remote:
        with_peer(
            b,
            lambda a=a, b=b: pl.semaphore_signal(
                barrier, inc=1, device_id=peer(a, b), device_id_type=MESH
            ),
        )

    for edge, b in ((0, -1), (lat_count - 1, 1)):

        @pl.when(lat == edge)
        def _(b=b):
            for a in (-1, 0, 1):
                slots[slot_of(a, b)] = jnp.zeros((CELLS, 128), jnp.bfloat16)

    loads[0].wait()
    loads[1].wait()
    loads[2].wait()
    cells = cells_ref[0]
    live = lax.broadcasted_iota(jnp.int32, cells.shape, 1) < count_ref[...]
    target = jnp.where(live, cells, -1)
    onehot = jnp.where(
        lax.broadcasted_iota(jnp.int32, (CELLS, cells.shape[1]), 0) == target, 1.0, 0.0
    ).astype(jnp.bfloat16)
    summed = lax.dot_general(
        onehot, obs_ref[0, 0], (((1,), (1,)), ((), ())), preferred_element_type=jnp.float32
    )
    high = summed.astype(jnp.bfloat16)
    low = (summed - high.astype(jnp.float32)).astype(jnp.bfloat16)
    slots[CENTRE] = jnp.concatenate([high, low], axis=1)

    lanes = lax.broadcasted_iota(jnp.int32, (64, 128), 1)
    low_mask = jnp.where(lanes < 64, 1.0, 0.0).astype(jnp.bfloat16)
    high_mask = jnp.where(lanes < 64, 0.0, 1.0).astype(jnp.bfloat16)

    loads[3].wait()
    loads[4].wait()
    enc = enc_ref[...]
    composite(enc, near_ref, composite_ref, 9, low_mask, high_mask)

    pl.semaphore_wait(barrier, jnp.where((lat == 0) | (lat == lat_count - 1), 5, 8))
    copies = []
    for a, b in remote:
        copies.append(
            (
                b,
                pltpu.make_async_remote_copy(
                    src_ref=slots.at[CENTRE],
                    dst_ref=slots.at[slot_of(-a, -b)],
                    send_sem=send_sems.at[slot_of(a, b)],
                    recv_sem=recv_sems.at[slot_of(-a, -b)],
                    device_id=peer(a, b),
                    device_id_type=MESH,
                ),
            )
        )
    for b, copy in copies:
        with_peer(b, copy.start)

    loads[5].wait()
    composite(enc, far_ref, composite_ref, 0, low_mask, high_mask)
    centre = slice(CENTRE * 64, CENTRE * 64 + 64)
    composite_ref[centre] = (
        composite_ref[centre].astype(jnp.float32) + enc.astype(jnp.float32)
    ).astype(jnp.bfloat16)

    for a, b in remote:
        arrival = pltpu.make_async_remote_copy(
            src_ref=slots.at[CENTRE],
            dst_ref=slots.at[slot_of(a, b)],
            send_sem=send_sems.at[slot_of(a, b)],
            recv_sem=recv_sems.at[slot_of(a, b)],
            device_id=peer(a, b),
            device_id_type=MESH,
        )
        with_peer(b, arrival.wait_recv)

    whole = [slots[i].astype(jnp.float32).reshape(LON, LAT, 128) for i in range(9)]
    lon_extended = [
        jnp.concatenate(
            [whole[slot_of(-1, b)][LON - 1 :], whole[slot_of(0, b)], whole[slot_of(1, b)][:1]], 0
        )
        for b in (-1, 0, 1)
    ]
    row = lax.broadcasted_iota(jnp.int32, (LON + 2, LAT, 128), 1)
    before = jnp.where(
        row == 0, pltpu.roll(lon_extended[0], 1, 1), pltpu.roll(lon_extended[1], 1, 1)
    )
    after = jnp.where(
        row == LAT - 1,
        pltpu.roll(lon_extended[2], LAT - 1, 1),
        pltpu.roll(lon_extended[1], LAT - 1, 1),
    )
    shifted = [before, lon_extended[1], after]
    taps = [piece.reshape(CELLS, 128) for piece in whole]
    for a in range(3):
        for b in range(3):
            taps.append(shifted[b][a : a + LON].reshape(CELLS, 128))
    left_half = lax.broadcasted_iota(jnp.int32, (CELLS, 128), 1) < 64
    columns = []
    for i in range(0, 18, 2):
        first, second = taps[i], taps[i + 1]
        highs = jnp.where(left_half, first, pltpu.roll(second, 64, 1))
        lows = jnp.where(left_half, pltpu.roll(first, 64, 1), second)
        columns.append(jnp.concatenate([highs, lows], axis=0).astype(jnp.bfloat16))
    lhs = jnp.concatenate(columns, axis=1)

    channels = enc.shape[1]
    for start in range(0, channels, CHUNK):
        block = slice(start, start + CHUNK)
        product = jnp.dot(lhs, composite_ref[:, block], preferred_element_type=jnp.float32)
        total = product[:CELLS] + product[CELLS:]
        total_ref[:, block] = total
        inner = 0.7978845608 * (total + 0.044715 * (total * total * total))
        activ_ref[:, block] = (0.5 * total * (1.0 + jnp.tanh(inner))).astype(jnp.bfloat16)

    loads[6].wait()
    activ = activ_ref[...]
    for start in range(0, channels, CHUNK):
        block = slice(start, start + CHUNK)
        mixed = jnp.dot(activ, mix_ref[:, block], preferred_element_type=jnp.float32)
        out_ref[:, :, block] = (
            (total_ref[:, block] + mixed).astype(jnp.bfloat16).reshape(LON, LAT, CHUNK)
        )

    for b, copy in copies:
        with_peer(b, copy.wait_send)


def on_device(
    lon_count,
    lat_count,
    obs_rows,
    obs_cells,
    obs_counts,
    enc_weight,
    near_kernel_weight,
    far_kernel_weight,
    mix_weight,
):
    channels = mix_weight.shape[0]
    operands = (
        jnp.swapaxes(obs_rows, 2, 3),
        obs_cells,
        obs_counts,
        enc_weight,
        near_kernel_weight,
        far_kernel_weight,
        mix_weight,
    )
    return pl.pallas_call(
        functools.partial(kernel, lon_count, lat_count),
        out_shape=jax.ShapeDtypeStruct((LON, LAT, channels), jnp.bfloat16),
        in_specs=[pl.BlockSpec(memory_space=pltpu.HBM)] * len(operands),
        out_specs=pl.BlockSpec(memory_space=pltpu.VMEM),
        scratch_shapes=[pltpu.VMEM(array.shape, array.dtype) for array in operands]
        + [
            pltpu.VMEM((9, CELLS, 128), jnp.bfloat16),
            pltpu.VMEM((18 * 64, channels), jnp.bfloat16),
            pltpu.VMEM((CELLS, channels), jnp.float32),
            pltpu.VMEM((CELLS, channels), jnp.bfloat16),
            pltpu.SemaphoreType.DMA((7,)),
            pltpu.SemaphoreType.DMA((9,)),
            pltpu.SemaphoreType.DMA((9,)),
        ],
        compiler_params=pltpu.CompilerParams(collective_id=0, has_side_effects=True),
    )(*operands)


def solution(mesh):
    return jax.shard_map(
        functools.partial(on_device, mesh.shape["lon"], mesh.shape["lat"]),
        mesh=mesh,
        in_specs=(
            P("lon", "lat", None, None),
            P("lon", "lat", None),
            P("lon", "lat"),
            P(),
            P(),
            P(),
            P(),
        ),
        out_specs=P("lon", "lat", None),
        check_vma=False,
    )
```

```python
import functools

import jax
import jax.numpy as jnp
from jax import lax
from jax.experimental import pallas as pl
from jax.experimental.pallas import tpu as pltpu
from jax.sharding import PartitionSpec as P

LON = 8
LAT = 8
CELLS = LON * LAT
MESH = pl.DeviceIdType.MESH
OFFSETS = [(a, b) for a in (-1, 0, 1) for b in (-1, 0, 1)]
CENTRE = 4
CHUNK = 256


def slot_of(a, b):
    return (a + 1) * 3 + (b + 1)


def composite(enc, weight_ref, composite_ref, base, low_mask, high_mask):
    features, channels = enc.shape
    zero = jnp.zeros((features, 128), jnp.bfloat16)

    def tap(t, carry):
        taps = weight_ref[t // 3, t % 3]
        for start in range(0, channels, CHUNK):
            left = taps[:, start : start + 128]
            right = taps[:, start + 128 : start + 256]
            blocks = jnp.concatenate(
                [
                    jnp.concatenate([left * low_mask, zero], axis=1),
                    jnp.concatenate([left * high_mask, zero], axis=1),
                    jnp.concatenate([zero, right * low_mask], axis=1),
                    jnp.concatenate([zero, right * high_mask], axis=1),
                ],
                axis=0,
            )
            product = jnp.dot(
                enc[:, start : start + CHUNK], blocks, preferred_element_type=jnp.float32
            )
            row = pl.multiple_of((base + t) * features, features)
            composite_ref[pl.ds(row, features), start : start + CHUNK] = product.astype(
                jnp.bfloat16
            )
        return carry

    lax.fori_loop(0, 9, tap, 0)


def kernel(
    lon_count,
    lat_count,
    obs_hbm,
    cells_hbm,
    count_hbm,
    enc_hbm,
    near_hbm,
    far_hbm,
    total_ref,
    activ_ref,
    obs_ref,
    cells_ref,
    count_ref,
    enc_ref,
    near_ref,
    far_ref,
    slots,
    composite_ref,
    local_sems,
    send_sems,
    recv_sems,
):
    pairs = [
        (obs_hbm, obs_ref),
        (cells_hbm, cells_ref),
        (count_hbm, count_ref),
        (enc_hbm, enc_ref),
        (near_hbm, near_ref),
        (far_hbm, far_ref),
    ]
    loads = [
        pltpu.make_async_copy(source, target, local_sems.at[i])
        for i, (source, target) in enumerate(pairs)
    ]
    for load in loads[:3]:
        load.start()

    lon = lax.axis_index("lon")
    lat = lax.axis_index("lat")

    def peer(a, b):
        return {"lon": lax.rem(lon + a + lon_count, lon_count), "lat": lat + b}

    def with_peer(b, body):
        if b == 0:
            body()
        elif b < 0:
            pl.when(lat > 0)(body)
        else:
            pl.when(lat < lat_count - 1)(body)

    remote = [(a, b) for a, b in OFFSETS if (a, b) != (0, 0)]
    barrier = pltpu.get_barrier_semaphore()
    for a, b in remote:
        with_peer(
            b,
            lambda a=a, b=b: pl.semaphore_signal(
                barrier, inc=1, device_id=peer(a, b), device_id_type=MESH
            ),
        )

    for edge, b in ((0, -1), (lat_count - 1, 1)):

        @pl.when(lat == edge)
        def _(b=b):
            for a in (-1, 0, 1):
                slots[slot_of(a, b)] = jnp.zeros((CELLS, 128), jnp.bfloat16)

    loads[0].wait()
    loads[1].wait()
    loads[2].wait()
    for load in loads[3:]:
        load.start()
    cells = cells_ref[0]
    live = lax.broadcasted_iota(jnp.int32, cells.shape, 1) < count_ref[...]
    target = jnp.where(live, cells, -1)
    onehot = jnp.where(
        lax.broadcasted_iota(jnp.int32, (CELLS, cells.shape[1]), 0) == target, 1.0, 0.0
    ).astype(jnp.bfloat16)
    summed = lax.dot_general(
        onehot, obs_ref[0, 0], (((1,), (1,)), ((), ())), preferred_element_type=jnp.float32
    )
    high = summed.astype(jnp.bfloat16)
    low = (summed - high.astype(jnp.float32)).astype(jnp.bfloat16)
    slots[CENTRE] = jnp.concatenate([high, low], axis=1)

    pl.semaphore_wait(barrier, jnp.where((lat == 0) | (lat == lat_count - 1), 5, 8))
    copies = []
    for a, b in remote:
        copies.append(
            (
                b,
                pltpu.make_async_remote_copy(
                    src_ref=slots.at[CENTRE],
                    dst_ref=slots.at[slot_of(-a, -b)],
                    send_sem=send_sems.at[slot_of(a, b)],
                    recv_sem=recv_sems.at[slot_of(-a, -b)],
                    device_id=peer(a, b),
                    device_id_type=MESH,
                ),
            )
        )
    for b, copy in copies:
        with_peer(b, copy.start)

    lanes = lax.broadcasted_iota(jnp.int32, (64, 128), 1)
    low_mask = jnp.where(lanes < 64, 1.0, 0.0).astype(jnp.bfloat16)
    high_mask = jnp.where(lanes < 64, 0.0, 1.0).astype(jnp.bfloat16)

    loads[3].wait()
    loads[4].wait()
    enc = enc_ref[...]
    composite(enc, near_ref, composite_ref, 9, low_mask, high_mask)

    loads[5].wait()
    composite(enc, far_ref, composite_ref, 0, low_mask, high_mask)
    centre = slice(CENTRE * 64, CENTRE * 64 + 64)
    composite_ref[centre] = (
        composite_ref[centre].astype(jnp.float32) + enc.astype(jnp.float32)
    ).astype(jnp.bfloat16)

    for a, b in remote:
        arrival = pltpu.make_async_remote_copy(
            src_ref=slots.at[CENTRE],
            dst_ref=slots.at[slot_of(a, b)],
            send_sem=send_sems.at[slot_of(a, b)],
            recv_sem=recv_sems.at[slot_of(a, b)],
            device_id=peer(a, b),
            device_id_type=MESH,
        )
        with_peer(b, arrival.wait_recv)

    whole = [slots[i].astype(jnp.float32).reshape(LON, LAT, 128) for i in range(9)]
    lon_extended = [
        jnp.concatenate(
            [whole[slot_of(-1, b)][LON - 1 :], whole[slot_of(0, b)], whole[slot_of(1, b)][:1]], 0
        )
        for b in (-1, 0, 1)
    ]
    row = lax.broadcasted_iota(jnp.int32, (LON + 2, LAT, 128), 1)
    before = jnp.where(
        row == 0, pltpu.roll(lon_extended[0], 1, 1), pltpu.roll(lon_extended[1], 1, 1)
    )
    after = jnp.where(
        row == LAT - 1,
        pltpu.roll(lon_extended[2], LAT - 1, 1),
        pltpu.roll(lon_extended[1], LAT - 1, 1),
    )
    shifted = [before, lon_extended[1], after]
    taps = [piece.reshape(CELLS, 128) for piece in whole]
    for a in range(3):
        for b in range(3):
            taps.append(shifted[b][a : a + LON].reshape(CELLS, 128))
    left_half = lax.broadcasted_iota(jnp.int32, (CELLS, 128), 1) < 64
    columns = []
    for i in range(0, 18, 2):
        first, second = taps[i], taps[i + 1]
        highs = jnp.where(left_half, first, pltpu.roll(second, 64, 1))
        lows = jnp.where(left_half, pltpu.roll(first, 64, 1), second)
        columns.append(jnp.concatenate([highs, lows], axis=0).astype(jnp.bfloat16))
    lhs = jnp.concatenate(columns, axis=1)

    channels = enc.shape[1]
    for start in range(0, channels, CHUNK):
        block = slice(start, start + CHUNK)
        product = jnp.dot(lhs, composite_ref[:, block], preferred_element_type=jnp.float32)
        total = product[:CELLS] + product[CELLS:]
        total_ref[:, block] = total
        inner = 0.7978845608 * (total + 0.044715 * (total * total * total))
        activ_ref[:, block] = (0.5 * total * (1.0 + jnp.tanh(inner))).astype(jnp.bfloat16)

    for b, copy in copies:
        with_peer(b, copy.wait_send)


def on_device(
    lon_count,
    lat_count,
    obs_rows,
    obs_cells,
    obs_counts,
    enc_weight,
    near_kernel_weight,
    far_kernel_weight,
    mix_weight,
):
    channels = mix_weight.shape[0]
    operands = (
        jnp.swapaxes(obs_rows, 2, 3),
        obs_cells,
        obs_counts,
        enc_weight,
        near_kernel_weight,
        far_kernel_weight,
    )
    total, activ = pl.pallas_call(
        functools.partial(kernel, lon_count, lat_count),
        out_shape=[
            jax.ShapeDtypeStruct((CELLS, channels), jnp.float32),
            jax.ShapeDtypeStruct((CELLS, channels), jnp.bfloat16),
        ],
        in_specs=[pl.BlockSpec(memory_space=pltpu.HBM)] * len(operands),
        out_specs=[pl.BlockSpec(memory_space=pltpu.VMEM)] * 2,
        scratch_shapes=[pltpu.VMEM(array.shape, array.dtype) for array in operands]
        + [
            pltpu.VMEM((9, CELLS, 128), jnp.bfloat16),
            pltpu.VMEM((18 * 64, channels), jnp.bfloat16),
            pltpu.SemaphoreType.DMA((6,)),
            pltpu.SemaphoreType.DMA((9,)),
            pltpu.SemaphoreType.DMA((9,)),
        ],
        compiler_params=pltpu.CompilerParams(
            collective_id=0, has_side_effects=True, vmem_limit_bytes=24 * 1024 * 1024
        ),
    )(
        *[
            array if array is obs_counts else pltpu.with_memory_space_constraint(array, pltpu.HBM)
            for array in operands
        ]
    )
    mixed = jnp.dot(activ, mix_weight, preferred_element_type=jnp.float32)
    return (total + mixed).astype(jnp.bfloat16).reshape(LON, LAT, channels)


def solution(mesh):
    return jax.shard_map(
        functools.partial(on_device, mesh.shape["lon"], mesh.shape["lat"]),
        mesh=mesh,
        in_specs=(
            P("lon", "lat", None, None),
            P("lon", "lat", None),
            P("lon", "lat"),
            P(),
            P(),
            P(),
            P(),
        ),
        out_specs=P("lon", "lat", None),
        check_vma=False,
    )
```

```python
import functools

import jax
import jax.numpy as jnp
from jax import lax
from jax.experimental import pallas as pl
from jax.experimental.pallas import tpu as pltpu
from jax.sharding import PartitionSpec as P

LON = 8
LAT = 8
CELLS = LON * LAT
HALF = CELLS // 2
MESH = pl.DeviceIdType.MESH
OFFSETS = [(a, b) for a in (-1, 0, 1) for b in (-1, 0, 1)]
CENTRE = 4
CHUNK = 256


def slot_of(a, b):
    return (a + 1) * 3 + (b + 1)


def composite(enc, weight_ref, composite_ref, base, low_mask, high_mask):
    features, channels = enc.shape
    zero = jnp.zeros((features, 128), jnp.bfloat16)

    def tap(t, carry):
        taps = weight_ref[t // 3, t % 3]
        for start in range(0, channels, CHUNK):
            left = taps[:, start : start + 128]
            right = taps[:, start + 128 : start + 256]
            blocks = jnp.concatenate(
                [
                    jnp.concatenate([left * low_mask, zero], axis=1),
                    jnp.concatenate([left * high_mask, zero], axis=1),
                    jnp.concatenate([zero, right * low_mask], axis=1),
                    jnp.concatenate([zero, right * high_mask], axis=1),
                ],
                axis=0,
            )
            product = jnp.dot(
                enc[:, start : start + CHUNK], blocks, preferred_element_type=jnp.float32
            )
            row = pl.multiple_of((base + t) * features, features)
            composite_ref[pl.ds(row, features), start : start + CHUNK] = product.astype(
                jnp.bfloat16
            )
        return carry

    lax.fori_loop(0, 9, tap, 0)


def kernel(
    lon_count,
    lat_count,
    obs_hbm,
    cells_hbm,
    count_hbm,
    enc_hbm,
    near_hbm,
    far_hbm,
    total_ref,
    activ_ref,
    obs_ref,
    cells_ref,
    count_ref,
    enc_ref,
    near_ref,
    far_ref,
    slots,
    composite_ref,
    local_sems,
    send_sems,
    recv_sems,
):
    pairs = [
        (obs_hbm, obs_ref),
        (cells_hbm, cells_ref),
        (count_hbm, count_ref),
        (enc_hbm, enc_ref),
        (near_hbm, near_ref),
        (far_hbm, far_ref),
    ]
    loads = [
        pltpu.make_async_copy(source, target, local_sems.at[i])
        for i, (source, target) in enumerate(pairs)
    ]
    for load in loads[:3]:
        load.start()

    lon = lax.axis_index("lon")
    lat = lax.axis_index("lat")

    def peer(a, b):
        return {"lon": lax.rem(lon + a + lon_count, lon_count), "lat": lat + b}

    def with_peer(b, body):
        if b == 0:
            body()
        elif b < 0:
            pl.when(lat > 0)(body)
        else:
            pl.when(lat < lat_count - 1)(body)

    remote = [(a, b) for a in (1, -1, 0) for b in (-1, 0, 1) if (a, b) != (0, 0)]
    barrier = pltpu.get_barrier_semaphore()
    for a, b in remote:
        with_peer(
            b,
            lambda a=a, b=b: pl.semaphore_signal(
                barrier, inc=1, device_id=peer(a, b), device_id_type=MESH
            ),
        )

    for edge, b in ((0, -1), (lat_count - 1, 1)):

        @pl.when(lat == edge)
        def _(b=b):
            for a in (-1, 0, 1):
                slots[slot_of(a, b)] = jnp.zeros((HALF, 128), jnp.bfloat16)

    loads[0].wait()
    loads[1].wait()
    loads[2].wait()
    for load in loads[3:]:
        load.start()
    cells = cells_ref[0]
    live = lax.broadcasted_iota(jnp.int32, cells.shape, 1) < count_ref[...]
    target = jnp.where(live, cells, -1)
    onehot = jnp.where(
        lax.broadcasted_iota(jnp.int32, (CELLS, cells.shape[1]), 0) == target, 1.0, 0.0
    ).astype(jnp.bfloat16)
    summed = lax.dot_general(
        onehot, obs_ref[0, 0], (((1,), (1,)), ((), ())), preferred_element_type=jnp.float32
    )
    slots[CENTRE] = jnp.concatenate([summed[:HALF], summed[HALF:]], axis=1).astype(jnp.bfloat16)

    pl.semaphore_wait(barrier, jnp.where((lat == 0) | (lat == lat_count - 1), 5, 8))
    copies = []
    for a, b in remote:
        copies.append(
            (
                b,
                pltpu.make_async_remote_copy(
                    src_ref=slots.at[CENTRE],
                    dst_ref=slots.at[slot_of(-a, -b)],
                    send_sem=send_sems.at[slot_of(a, b)],
                    recv_sem=recv_sems.at[slot_of(-a, -b)],
                    device_id=peer(a, b),
                    device_id_type=MESH,
                ),
            )
        )
    for b, copy in copies:
        with_peer(b, copy.start)

    lanes = lax.broadcasted_iota(jnp.int32, (64, 128), 1)
    low_mask = jnp.where(lanes < 64, 1.0, 0.0).astype(jnp.bfloat16)
    high_mask = jnp.where(lanes < 64, 0.0, 1.0).astype(jnp.bfloat16)

    loads[3].wait()
    loads[4].wait()
    enc = enc_ref[...]
    composite(enc, near_ref, composite_ref, 9, low_mask, high_mask)

    loads[5].wait()
    composite(enc, far_ref, composite_ref, 0, low_mask, high_mask)
    centre = slice(CENTRE * 64, CENTRE * 64 + 64)
    composite_ref[centre] = (
        composite_ref[centre].astype(jnp.float32) + enc.astype(jnp.float32)
    ).astype(jnp.bfloat16)

    for a, b in remote:
        arrival = pltpu.make_async_remote_copy(
            src_ref=slots.at[CENTRE],
            dst_ref=slots.at[slot_of(a, b)],
            send_sem=send_sems.at[slot_of(a, b)],
            recv_sem=recv_sems.at[slot_of(a, b)],
            device_id=peer(a, b),
            device_id_type=MESH,
        )
        with_peer(b, arrival.wait_recv)

    half_lon = LON // 2
    whole = [slots[i].astype(jnp.float32).reshape(half_lon, LAT, 128) for i in range(9)]
    left_half = lax.broadcasted_iota(jnp.int32, (1, LAT, 128), 2) < 64
    lon_extended = []
    for b in (-1, 0, 1):
        minus, own, plus = [whole[slot_of(a, b)] for a in (-1, 0, 1)]
        first = jnp.where(left_half, own[half_lon - 1 :], minus[half_lon - 1 :])
        last = jnp.where(left_half, plus[:1], own[:1])
        lon_extended.append(
            jnp.concatenate([pltpu.roll(first, 64, 2), own, pltpu.roll(last, 64, 2)], 0)
        )
    row = lax.broadcasted_iota(jnp.int32, (half_lon + 2, LAT, 128), 1)
    before = jnp.where(
        row == 0, pltpu.roll(lon_extended[0], 1, 1), pltpu.roll(lon_extended[1], 1, 1)
    )
    after = jnp.where(
        row == LAT - 1,
        pltpu.roll(lon_extended[2], LAT - 1, 1),
        pltpu.roll(lon_extended[1], LAT - 1, 1),
    )
    shifted = [before, lon_extended[1], after]
    taps = [piece.reshape(HALF, 128) for piece in whole]
    for a in range(3):
        for b in range(3):
            taps.append(shifted[b][a : a + half_lon].reshape(HALF, 128))
    left_half = lax.broadcasted_iota(jnp.int32, (HALF, 128), 1) < 64
    columns = []
    for i in range(0, 18, 2):
        first, second = taps[i], taps[i + 1]
        upper = jnp.where(left_half, first, pltpu.roll(second, 64, 1))
        lower = jnp.where(left_half, pltpu.roll(first, 64, 1), second)
        columns.append(jnp.concatenate([upper, lower], axis=0).astype(jnp.bfloat16))
    lhs = jnp.concatenate(columns, axis=1)

    channels = enc.shape[1]
    for start in range(0, channels, CHUNK):
        block = slice(start, start + CHUNK)
        total = jnp.dot(lhs, composite_ref[:, block], preferred_element_type=jnp.float32)
        total_ref[:, block] = total
        inner = 0.7978845608 * (total + 0.044715 * (total * total * total))
        activ_ref[:, block] = (0.5 * total * (1.0 + jnp.tanh(inner))).astype(jnp.bfloat16)

    for b, copy in copies:
        with_peer(b, copy.wait_send)


def on_device(
    lon_count,
    lat_count,
    obs_rows,
    obs_cells,
    obs_counts,
    enc_weight,
    near_kernel_weight,
    far_kernel_weight,
    mix_weight,
):
    channels = mix_weight.shape[0]
    operands = (
        jnp.swapaxes(obs_rows, 2, 3),
        obs_cells,
        obs_counts,
        enc_weight,
        near_kernel_weight,
        far_kernel_weight,
    )
    total, activ = pl.pallas_call(
        functools.partial(kernel, lon_count, lat_count),
        out_shape=[
            jax.ShapeDtypeStruct((CELLS, channels), jnp.float32),
            jax.ShapeDtypeStruct((CELLS, channels), jnp.bfloat16),
        ],
        in_specs=[pl.BlockSpec(memory_space=pltpu.HBM)] * len(operands),
        out_specs=[pl.BlockSpec(memory_space=pltpu.VMEM)] * 2,
        scratch_shapes=[pltpu.VMEM(array.shape, array.dtype) for array in operands]
        + [
            pltpu.VMEM((9, HALF, 128), jnp.bfloat16),
            pltpu.VMEM((18 * 64, channels), jnp.bfloat16),
            pltpu.SemaphoreType.DMA((6,)),
            pltpu.SemaphoreType.DMA((9,)),
            pltpu.SemaphoreType.DMA((9,)),
        ],
        compiler_params=pltpu.CompilerParams(
            collective_id=0, has_side_effects=True, vmem_limit_bytes=24 * 1024 * 1024
        ),
    )(
        *[
            array if array is obs_counts else pltpu.with_memory_space_constraint(array, pltpu.HBM)
            for array in operands
        ]
    )
    mixed = jnp.dot(activ, mix_weight, preferred_element_type=jnp.float32)
    return (total + mixed).astype(jnp.bfloat16).reshape(LON, LAT, channels)


def solution(mesh):
    return jax.shard_map(
        functools.partial(on_device, mesh.shape["lon"], mesh.shape["lat"]),
        mesh=mesh,
        in_specs=(
            P("lon", "lat", None, None),
            P("lon", "lat", None),
            P("lon", "lat"),
            P(),
            P(),
            P(),
            P(),
        ),
        out_specs=P("lon", "lat", None),
        check_vma=False,
    )
```

```python
import functools

import jax
import jax.numpy as jnp
from jax import lax
from jax.experimental import pallas as pl
from jax.experimental.pallas import tpu as pltpu
from jax.sharding import PartitionSpec as P

LON = 8
LAT = 8
CELLS = LON * LAT
HALF = CELLS // 2
MESH = pl.DeviceIdType.MESH
OFFSETS = [(a, b) for a in (-1, 0, 1) for b in (-1, 0, 1)]
CENTRE = 4
OBS_PARTS = 4
CHUNK = 256


def slot_of(a, b):
    return (a + 1) * 3 + (b + 1)


def composite(enc, weight_ref, composite_ref, base, low_mask, high_mask):
    features, channels = enc.shape
    zero = jnp.zeros((features, 128), jnp.bfloat16)

    def tap(t, carry):
        taps = weight_ref[t // 3, t % 3]
        for start in range(0, channels, CHUNK):
            left = taps[:, start : start + 128]
            right = taps[:, start + 128 : start + 256]
            blocks = jnp.concatenate(
                [
                    jnp.concatenate([left * low_mask, zero], axis=1),
                    jnp.concatenate([left * high_mask, zero], axis=1),
                    jnp.concatenate([zero, right * low_mask], axis=1),
                    jnp.concatenate([zero, right * high_mask], axis=1),
                ],
                axis=0,
            )
            product = jnp.dot(
                enc[:, start : start + CHUNK], blocks, preferred_element_type=jnp.float32
            )
            row = pl.multiple_of((base + t) * features, features)
            composite_ref[pl.ds(row, features), start : start + CHUNK] = product.astype(
                jnp.bfloat16
            )
        return carry

    lax.fori_loop(0, 9, tap, 0)


def kernel(
    lon_count,
    lat_count,
    obs_hbm,
    cells_hbm,
    count_hbm,
    enc_hbm,
    near_hbm,
    far_hbm,
    mix_hbm,
    total_ref,
    activ_ref,
    mix_ref,
    obs_ref,
    cells_ref,
    count_ref,
    enc_ref,
    near_ref,
    far_ref,
    slots,
    composite_ref,
    local_sems,
    obs_sems,
    send_sems,
    recv_sems,
    ready_sem,
):
    pairs = [
        (obs_hbm, obs_ref),
        (cells_hbm, cells_ref),
        (count_hbm, count_ref),
        (enc_hbm, enc_ref),
        (near_hbm, near_ref),
        (far_hbm, far_ref),
        (mix_hbm, mix_ref),
    ]
    loads = [
        pltpu.make_async_copy(source, target, local_sems.at[i])
        for i, (source, target) in enumerate(pairs)
    ]
    features = obs_ref.shape[2] // OBS_PARTS
    obs_loads = []
    for i in range(OBS_PARTS):
        part = (0, 0, slice(i * features, (i + 1) * features))
        obs_loads.append(
            pltpu.make_async_copy(obs_hbm.at[part], obs_ref.at[part], obs_sems.at[i])
        )
    for load in obs_loads + loads[1:3]:
        load.start()

    lon = lax.axis_index("lon")
    lat = lax.axis_index("lat")

    def peer(a, b):
        return {"lon": lax.rem(lon + a + lon_count, lon_count), "lat": lat + b}

    def with_peer(b, body):
        if b == 0:
            body()
        elif b < 0:
            pl.when(lat > 0)(body)
        else:
            pl.when(lat < lat_count - 1)(body)

    remote = [(a, b) for a in (1, 0, -1) for b in (-1, 0, 1) if (a, b) != (0, 0)]
    barrier = pltpu.get_barrier_semaphore()
    for a, b in remote:
        if a < 1:
            with_peer(
                b,
                lambda a=a, b=b: pl.semaphore_signal(
                    barrier, inc=1, device_id=peer(a, b), device_id_type=MESH
                ),
            )

    for edge, b in ((0, -1), (lat_count - 1, 1)):

        @pl.when(lat == edge)
        def _(b=b):
            for a in (-1, 0, 1):
                slots[slot_of(a, b)] = jnp.zeros((HALF, 128), jnp.bfloat16)

    for load in obs_loads:
        load.wait()
    loads[1].wait()
    loads[2].wait()
    for load in loads[3:]:
        load.start()
    cells = cells_ref[0]
    live = lax.broadcasted_iota(jnp.int32, cells.shape, 1) < count_ref[...]
    target = jnp.where(live, cells, -1)
    onehot = jnp.where(
        lax.broadcasted_iota(jnp.int32, (CELLS, cells.shape[1]), 0) == target, 1.0, 0.0
    ).astype(jnp.bfloat16)
    summed = lax.dot_general(
        onehot, obs_ref[0, 0], (((1,), (1,)), ((), ())), preferred_element_type=jnp.float32
    )
    slots[CENTRE] = jnp.concatenate([summed[:HALF], summed[HALF:]], axis=1).astype(jnp.bfloat16)

    at_edge = (lat == 0) | (lat == lat_count - 1)
    pl.semaphore_wait(barrier, jnp.where(at_edge, 3, 5))
    copies = []
    for a, b in remote:
        copies.append(
            (
                a,
                b,
                pltpu.make_async_remote_copy(
                    src_ref=slots.at[CENTRE],
                    dst_ref=slots.at[slot_of(-a, -b)],
                    send_sem=send_sems.at[slot_of(a, b)],
                    recv_sem=recv_sems.at[slot_of(-a, -b)],
                    device_id=peer(a, b),
                    device_id_type=MESH,
                ),
            )
        )
    for a, b, copy in copies:
        if a >= 0:
            with_peer(b, copy.start)
    for b in (-1, 0, 1):
        with_peer(
            b,
            lambda b=b: pl.semaphore_signal(
                ready_sem, inc=1, device_id=peer(1, b), device_id_type=MESH
            ),
        )

    lanes = lax.broadcasted_iota(jnp.int32, (64, 128), 1)
    low_mask = jnp.where(lanes < 64, 1.0, 0.0).astype(jnp.bfloat16)
    high_mask = jnp.where(lanes < 64, 0.0, 1.0).astype(jnp.bfloat16)

    loads[3].wait()
    loads[4].wait()
    enc = enc_ref[...]
    composite(enc, near_ref, composite_ref, 9, low_mask, high_mask)

    loads[5].wait()
    composite(enc, far_ref, composite_ref, 0, low_mask, high_mask)
    centre = slice(CENTRE * 64, CENTRE * 64 + 64)
    composite_ref[centre] = (
        composite_ref[centre].astype(jnp.float32) + enc.astype(jnp.float32)
    ).astype(jnp.bfloat16)

    pl.semaphore_wait(ready_sem, jnp.where(at_edge, 2, 3))
    for a, b, copy in copies:
        if a < 0:
            with_peer(b, copy.start)

    for a, b in remote:
        arrival = pltpu.make_async_remote_copy(
            src_ref=slots.at[CENTRE],
            dst_ref=slots.at[slot_of(a, b)],
            send_sem=send_sems.at[slot_of(a, b)],
            recv_sem=recv_sems.at[slot_of(a, b)],
            device_id=peer(a, b),
            device_id_type=MESH,
        )
        with_peer(b, arrival.wait_recv)

    half_lon = LON // 2
    whole = [slots[i].astype(jnp.float32).reshape(half_lon, LAT, 128) for i in range(9)]
    left_half = lax.broadcasted_iota(jnp.int32, (1, LAT, 128), 2) < 64
    lon_extended = []
    for b in (-1, 0, 1):
        minus, own, plus = [whole[slot_of(a, b)] for a in (-1, 0, 1)]
        first = jnp.where(left_half, own[half_lon - 1 :], minus[half_lon - 1 :])
        last = jnp.where(left_half, plus[:1], own[:1])
        lon_extended.append(
            jnp.concatenate([pltpu.roll(first, 64, 2), own, pltpu.roll(last, 64, 2)], 0)
        )
    row = lax.broadcasted_iota(jnp.int32, (half_lon + 2, LAT, 128), 1)
    before = jnp.where(
        row == 0, pltpu.roll(lon_extended[0], 1, 1), pltpu.roll(lon_extended[1], 1, 1)
    )
    after = jnp.where(
        row == LAT - 1,
        pltpu.roll(lon_extended[2], LAT - 1, 1),
        pltpu.roll(lon_extended[1], LAT - 1, 1),
    )
    shifted = [before, lon_extended[1], after]
    taps = [piece.reshape(HALF, 128) for piece in whole]
    for a in range(3):
        for b in range(3):
            taps.append(shifted[b][a : a + half_lon].reshape(HALF, 128))
    left_half = lax.broadcasted_iota(jnp.int32, (HALF, 128), 1) < 64
    columns = []
    for i in range(0, 18, 2):
        first, second = taps[i], taps[i + 1]
        upper = jnp.where(left_half, first, pltpu.roll(second, 64, 1))
        lower = jnp.where(left_half, pltpu.roll(first, 64, 1), second)
        columns.append(jnp.concatenate([upper, lower], axis=0).astype(jnp.bfloat16))
    lhs = jnp.concatenate(columns, axis=1)

    channels = enc.shape[1]
    for start in range(0, channels, CHUNK):
        block = slice(start, start + CHUNK)
        total = jnp.dot(lhs, composite_ref[:, block], preferred_element_type=jnp.float32)
        total_ref[:, block] = total
        inner = 0.7978845608 * (total + 0.044715 * (total * total * total))
        activ_ref[:, block] = (0.5 * total * (1.0 + jnp.tanh(inner))).astype(jnp.bfloat16)

    loads[6].wait()
    for a, b, copy in copies:
        with_peer(b, copy.wait_send)


def on_device(
    lon_count,
    lat_count,
    obs_rows,
    obs_cells,
    obs_counts,
    enc_weight,
    near_kernel_weight,
    far_kernel_weight,
    mix_weight,
):
    channels = mix_weight.shape[0]
    operands = (
        jnp.swapaxes(obs_rows, 2, 3),
        obs_cells,
        obs_counts,
        enc_weight,
        near_kernel_weight,
        far_kernel_weight,
        mix_weight,
    )
    total, activ, mix = pl.pallas_call(
        functools.partial(kernel, lon_count, lat_count),
        out_shape=[
            jax.ShapeDtypeStruct((CELLS, channels), jnp.float32),
            jax.ShapeDtypeStruct((CELLS, channels), jnp.bfloat16),
            jax.ShapeDtypeStruct(mix_weight.shape, jnp.bfloat16),
        ],
        in_specs=[pl.BlockSpec(memory_space=pltpu.HBM)] * len(operands),
        out_specs=[pl.BlockSpec(memory_space=pltpu.VMEM)] * 3,
        scratch_shapes=[pltpu.VMEM(array.shape, array.dtype) for array in operands[:-1]]
        + [
            pltpu.VMEM((9, HALF, 128), jnp.bfloat16),
            pltpu.VMEM((18 * 64, channels), jnp.bfloat16),
            pltpu.SemaphoreType.DMA((7,)),
            pltpu.SemaphoreType.DMA((OBS_PARTS,)),
            pltpu.SemaphoreType.DMA((9,)),
            pltpu.SemaphoreType.DMA((9,)),
            pltpu.SemaphoreType.REGULAR,
        ],
        compiler_params=pltpu.CompilerParams(
            collective_id=0, has_side_effects=True, vmem_limit_bytes=24 * 1024 * 1024
        ),
    )(
        *[
            array if array is obs_counts else pltpu.with_memory_space_constraint(array, pltpu.HBM)
            for array in operands
        ]
    )
    mixed = jnp.dot(activ, mix, preferred_element_type=jnp.float32)
    return (total + mixed).astype(jnp.bfloat16).reshape(LON, LAT, channels)


def solution(mesh):
    return jax.shard_map(
        functools.partial(on_device, mesh.shape["lon"], mesh.shape["lat"]),
        mesh=mesh,
        in_specs=(
            P("lon", "lat", None, None),
            P("lon", "lat", None),
            P("lon", "lat"),
            P(),
            P(),
            P(),
            P(),
        ),
        out_specs=P("lon", "lat", None),
        check_vma=False,
    )
```

```python
import functools

import jax
import jax.numpy as jnp
from jax import lax
from jax.experimental import pallas as pl
from jax.experimental.pallas import tpu as pltpu
from jax.sharding import PartitionSpec as P

LON = 8
LAT = 8
CELLS = LON * LAT
HALF = CELLS // 2
MESH = pl.DeviceIdType.MESH
OFFSETS = [(a, b) for a in (-1, 0, 1) for b in (-1, 0, 1)]
CENTRE = 4
OBS_PARTS = 4
CHUNK = 256


def slot_of(a, b):
    return (a + 1) * 3 + (b + 1)


def composite(enc, weight_ref, composite_ref, late, early, low_mask, high_mask):
    features, channels = enc.shape
    zero = jnp.zeros((features, 128), jnp.bfloat16)

    def tap(t, carry):
        taps = weight_ref[t // 3, t % 3]
        for start in range(0, channels, CHUNK):
            left = taps[:, start : start + 128]
            right = taps[:, start + 128 : start + 256]
            blocks = jnp.concatenate(
                [
                    jnp.concatenate([left * low_mask, zero], axis=1),
                    jnp.concatenate([left * high_mask, zero], axis=1),
                    jnp.concatenate([zero, right * low_mask], axis=1),
                    jnp.concatenate([zero, right * high_mask], axis=1),
                ],
                axis=0,
            )
            product = jnp.dot(
                enc[:, start : start + CHUNK], blocks, preferred_element_type=jnp.float32
            )
            row = pl.multiple_of((t + jnp.where(t < 3, late, early)) * features, features)
            composite_ref[pl.ds(row, features), start : start + CHUNK] = product.astype(
                jnp.bfloat16
            )
        return carry

    lax.fori_loop(0, 9, tap, 0)


def kernel(
    lon_count,
    lat_count,
    obs_hbm,
    cells_hbm,
    count_hbm,
    enc_hbm,
    near_hbm,
    far_hbm,
    mix_hbm,
    total_ref,
    activ_ref,
    mix_ref,
    obs_ref,
    cells_ref,
    count_ref,
    enc_ref,
    near_ref,
    far_ref,
    slots,
    composite_ref,
    local_sems,
    obs_sems,
    send_sems,
    recv_sems,
    ready_sem,
):
    pairs = [
        (obs_hbm, obs_ref),
        (cells_hbm, cells_ref),
        (count_hbm, count_ref),
        (enc_hbm, enc_ref),
        (near_hbm, near_ref),
        (far_hbm, far_ref),
        (mix_hbm, mix_ref),
    ]
    loads = [
        pltpu.make_async_copy(source, target, local_sems.at[i])
        for i, (source, target) in enumerate(pairs)
    ]
    features = obs_ref.shape[2] // OBS_PARTS
    obs_loads = []
    for i in range(OBS_PARTS):
        part = (0, 0, slice(i * features, (i + 1) * features))
        obs_loads.append(
            pltpu.make_async_copy(obs_hbm.at[part], obs_ref.at[part], obs_sems.at[i])
        )
    for load in obs_loads + loads[1:3]:
        load.start()

    lon = lax.axis_index("lon")
    lat = lax.axis_index("lat")

    def peer(a, b):
        return {"lon": lax.rem(lon + a + lon_count, lon_count), "lat": lat + b}

    def with_peer(b, body):
        if b == 0:
            body()
        elif b < 0:
            pl.when(lat > 0)(body)
        else:
            pl.when(lat < lat_count - 1)(body)

    remote = [(a, b) for a in (1, 0, -1) for b in (-1, 0, 1) if (a, b) != (0, 0)]
    barrier = pltpu.get_barrier_semaphore()
    for a, b in remote:
        if a < 0:
            with_peer(
                b,
                lambda a=a, b=b: pl.semaphore_signal(
                    barrier, inc=1, device_id=peer(a, b), device_id_type=MESH
                ),
            )

    for edge, b in ((0, -1), (lat_count - 1, 1)):

        @pl.when(lat == edge)
        def _(b=b):
            for a in (-1, 0, 1):
                slots[slot_of(a, b)] = jnp.zeros((HALF, 128), jnp.bfloat16)

    for load in obs_loads:
        load.wait()
    loads[1].wait()
    loads[2].wait()
    cells = cells_ref[0]
    live = lax.broadcasted_iota(jnp.int32, cells.shape, 1) < count_ref[...]
    target = jnp.where(live, cells, -1)
    onehot = jnp.where(
        lax.broadcasted_iota(jnp.int32, (CELLS, cells.shape[1]), 0) == target, 1.0, 0.0
    ).astype(jnp.bfloat16)
    summed = lax.dot_general(
        onehot, obs_ref[0, 0], (((1,), (1,)), ((), ())), preferred_element_type=jnp.float32
    )
    slots[CENTRE] = jnp.concatenate([summed[:HALF], summed[HALF:]], axis=1).astype(jnp.bfloat16)

    at_edge = (lat == 0) | (lat == lat_count - 1)
    pl.semaphore_wait(barrier, jnp.where(at_edge, 2, 3))
    copies = []
    for a, b in remote:
        copies.append(
            (
                a,
                b,
                pltpu.make_async_remote_copy(
                    src_ref=slots.at[CENTRE],
                    dst_ref=slots.at[slot_of(-a, -b)],
                    send_sem=send_sems.at[slot_of(a, b)],
                    recv_sem=recv_sems.at[slot_of(-a, -b)],
                    device_id=peer(a, b),
                    device_id_type=MESH,
                ),
            )
        )
    for a, b, copy in copies:
        if a > 0:
            with_peer(b, copy.start)
    for b in (-1, 0, 1):
        with_peer(
            b,
            lambda b=b: pl.semaphore_signal(
                ready_sem, inc=1, device_id=peer(1, b), device_id_type=MESH
            ),
        )
    for load in loads[3:]:
        load.start()

    lanes = lax.broadcasted_iota(jnp.int32, (64, 128), 1)
    low_mask = jnp.where(lanes < 64, 1.0, 0.0).astype(jnp.bfloat16)
    high_mask = jnp.where(lanes < 64, 0.0, 1.0).astype(jnp.bfloat16)

    loads[3].wait()
    loads[4].wait()
    enc = enc_ref[...]
    composite(enc, near_ref, composite_ref, 3, 9, low_mask, high_mask)

    loads[5].wait()
    composite(enc, far_ref, composite_ref, 0, 3, low_mask, high_mask)
    centre = slice((CENTRE + 3) * 64, (CENTRE + 4) * 64)
    composite_ref[centre] = (
        composite_ref[centre].astype(jnp.float32) + enc.astype(jnp.float32)
    ).astype(jnp.bfloat16)

    pl.semaphore_wait(ready_sem, jnp.where(at_edge, 2, 3))
    for a, b, copy in copies:
        if a < 1:
            with_peer(b, copy.start)

    def await_from(a):
        for c, b in remote:
            if c == a:
                arrival = pltpu.make_async_remote_copy(
                    src_ref=slots.at[CENTRE],
                    dst_ref=slots.at[slot_of(a, b)],
                    send_sem=send_sems.at[slot_of(a, b)],
                    recv_sem=recv_sems.at[slot_of(a, b)],
                    device_id=peer(a, b),
                    device_id_type=MESH,
                )
                with_peer(b, arrival.wait_recv)

    half_lon = LON // 2

    def blocks_of(a):
        return [
            slots[slot_of(a, b)].astype(jnp.float32).reshape(half_lon, LAT, 128)
            for b in (-1, 0, 1)
        ]

    left = lax.broadcasted_iota(jnp.int32, (1, LAT, 128), 2) < 64

    def lat_shifted(rows_of):
        row = lax.broadcasted_iota(jnp.int32, rows_of[0].shape, 1)
        before = jnp.where(row == 0, pltpu.roll(rows_of[0], 1, 1), pltpu.roll(rows_of[1], 1, 1))
        after = jnp.where(
            row == LAT - 1,
            pltpu.roll(rows_of[2], LAT - 1, 1),
            pltpu.roll(rows_of[1], LAT - 1, 1),
        )
        return [before, rows_of[1], after]

    def stacked(taps):
        taps = [tap.reshape(HALF, 128) for tap in taps]
        left_half = lax.broadcasted_iota(jnp.int32, (HALF, 128), 1) < 64
        columns = []
        for first, second in zip(taps[::2], taps[1::2]):
            upper = jnp.where(left_half, first, pltpu.roll(second, 64, 1))
            lower = jnp.where(left_half, pltpu.roll(first, 64, 1), second)
            columns.append(jnp.concatenate([upper, lower], axis=0).astype(jnp.bfloat16))
        return jnp.concatenate(columns, axis=1)

    channels = enc.shape[1]
    late_rows = 6 * 64

    await_from(0)
    await_from(1)
    own, plus = blocks_of(0), blocks_of(1)
    ahead = [
        jnp.concatenate([own[b], pltpu.roll(jnp.where(left, plus[b][:1], own[b][:1]), 64, 2)], 0)
        for b in range(3)
    ]
    ahead = lat_shifted(ahead)
    early = stacked(
        own
        + plus
        + [piece[:half_lon] for piece in ahead]
        + [piece[1 : 1 + half_lon] for piece in ahead]
    )
    for start in range(0, channels, CHUNK):
        block = slice(start, start + CHUNK)
        total_ref[:, block] = jnp.dot(
            early, composite_ref[late_rows:, block], preferred_element_type=jnp.float32
        )

    await_from(-1)
    own, minus = blocks_of(0), blocks_of(-1)
    behind = []
    for b in range(3):
        first = jnp.where(left, own[b][half_lon - 1 :], minus[b][half_lon - 1 :])
        behind.append(jnp.concatenate([pltpu.roll(first, 64, 2), own[b][: half_lon - 1]], 0))
    late = stacked(minus + lat_shifted(behind))
    for start in range(0, channels, CHUNK):
        block = slice(start, start + CHUNK)
        total = total_ref[:, block] + jnp.dot(
            late, composite_ref[:late_rows, block], preferred_element_type=jnp.float32
        )
        total_ref[:, block] = total
        inner = 0.7978845608 * (total + 0.044715 * (total * total * total))
        activ_ref[:, block] = (0.5 * total * (1.0 + jnp.tanh(inner))).astype(jnp.bfloat16)

    loads[6].wait()
    for a, b, copy in copies:
        with_peer(b, copy.wait_send)


def on_device(
    lon_count,
    lat_count,
    obs_rows,
    obs_cells,
    obs_counts,
    enc_weight,
    near_kernel_weight,
    far_kernel_weight,
    mix_weight,
):
    channels = mix_weight.shape[0]
    operands = (
        jnp.swapaxes(obs_rows, 2, 3),
        obs_cells,
        obs_counts,
        enc_weight,
        near_kernel_weight,
        far_kernel_weight,
        mix_weight,
    )
    total, activ, mix = pl.pallas_call(
        functools.partial(kernel, lon_count, lat_count),
        out_shape=[
            jax.ShapeDtypeStruct((CELLS, channels), jnp.float32),
            jax.ShapeDtypeStruct((CELLS, channels), jnp.bfloat16),
            jax.ShapeDtypeStruct(mix_weight.shape, jnp.bfloat16),
        ],
        in_specs=[pl.BlockSpec(memory_space=pltpu.HBM)] * len(operands),
        out_specs=[pl.BlockSpec(memory_space=pltpu.VMEM)] * 3,
        scratch_shapes=[pltpu.VMEM(array.shape, array.dtype) for array in operands[:-1]]
        + [
            pltpu.VMEM((9, HALF, 128), jnp.bfloat16),
            pltpu.VMEM((18 * 64, channels), jnp.bfloat16),
            pltpu.SemaphoreType.DMA((7,)),
            pltpu.SemaphoreType.DMA((OBS_PARTS,)),
            pltpu.SemaphoreType.DMA((9,)),
            pltpu.SemaphoreType.DMA((9,)),
            pltpu.SemaphoreType.REGULAR,
        ],
        compiler_params=pltpu.CompilerParams(
            collective_id=0, has_side_effects=True, vmem_limit_bytes=24 * 1024 * 1024
        ),
    )(
        *[
            array if array is obs_counts else pltpu.with_memory_space_constraint(array, pltpu.HBM)
            for array in operands
        ]
    )
    mixed = jnp.dot(activ, mix, preferred_element_type=jnp.float32)
    return (total + mixed).astype(jnp.bfloat16).reshape(LON, LAT, channels)


def solution(mesh):
    return jax.shard_map(
        functools.partial(on_device, mesh.shape["lon"], mesh.shape["lat"]),
        mesh=mesh,
        in_specs=(
            P("lon", "lat", None, None),
            P("lon", "lat", None),
            P("lon", "lat"),
            P(),
            P(),
            P(),
            P(),
        ),
        out_specs=P("lon", "lat", None),
        check_vma=False,
    )
```

```python
import functools

import jax
import jax.numpy as jnp
from jax import lax
from jax.experimental import pallas as pl
from jax.experimental.pallas import tpu as pltpu
from jax.sharding import PartitionSpec as P

LON = 8
LAT = 8
CELLS = LON * LAT
HALF = CELLS // 2
MESH = pl.DeviceIdType.MESH
OFFSETS = [(a, b) for a in (-1, 0, 1) for b in (-1, 0, 1)]
CENTRE = 4
OBS_PARTS = 4
CHUNK = 256


def slot_of(a, b):
    return (a + 1) * 3 + (b + 1)


def composite(enc, weight_ref, composite_ref, late, early, low_mask, high_mask):
    features, channels = enc.shape
    zero = jnp.zeros((features, 128), jnp.bfloat16)

    def tap(t, carry):
        taps = weight_ref[t // 3, t % 3]
        for start in range(0, channels, CHUNK):
            left = taps[:, start : start + 128]
            right = taps[:, start + 128 : start + 256]
            blocks = jnp.concatenate(
                [
                    jnp.concatenate([left * low_mask, zero], axis=1),
                    jnp.concatenate([left * high_mask, zero], axis=1),
                    jnp.concatenate([zero, right * low_mask], axis=1),
                    jnp.concatenate([zero, right * high_mask], axis=1),
                ],
                axis=0,
            )
            product = jnp.dot(
                enc[:, start : start + CHUNK], blocks, preferred_element_type=jnp.float32
            )
            row = pl.multiple_of((t + jnp.where(t < 3, late, early)) * features, features)
            composite_ref[pl.ds(row, features), start : start + CHUNK] = product.astype(
                jnp.bfloat16
            )
        return carry

    lax.fori_loop(0, 9, tap, 0)


def kernel(
    lon_count,
    lat_count,
    obs_hbm,
    cells_hbm,
    count_hbm,
    enc_hbm,
    near_hbm,
    far_hbm,
    mix_hbm,
    total_ref,
    activ_ref,
    mix_ref,
    obs_ref,
    cells_ref,
    count_ref,
    enc_ref,
    near_ref,
    far_ref,
    slots,
    composite_ref,
    local_sems,
    obs_sems,
    send_sems,
    recv_sems,
    ready_sem,
):
    pairs = [
        (obs_hbm, obs_ref),
        (cells_hbm, cells_ref),
        (count_hbm, count_ref),
        (enc_hbm, enc_ref),
        (near_hbm, near_ref),
        (far_hbm, far_ref),
        (mix_hbm, mix_ref),
    ]
    loads = [
        pltpu.make_async_copy(source, target, local_sems.at[i])
        for i, (source, target) in enumerate(pairs)
    ]
    features = obs_ref.shape[2] // OBS_PARTS
    obs_loads = []
    for i in range(OBS_PARTS):
        part = (0, 0, slice(i * features, (i + 1) * features))
        obs_loads.append(
            pltpu.make_async_copy(obs_hbm.at[part], obs_ref.at[part], obs_sems.at[i])
        )
    for load in loads[1:3] + obs_loads:
        load.start()

    lon = lax.axis_index("lon")
    lat = lax.axis_index("lat")

    def peer(a, b):
        return {"lon": lax.rem(lon + a + lon_count, lon_count), "lat": lat + b}

    def with_peer(b, body):
        if b == 0:
            body()
        elif b < 0:
            pl.when(lat > 0)(body)
        else:
            pl.when(lat < lat_count - 1)(body)

    remote = [(a, b) for a in (1, 0, -1) for b in (-1, 0, 1) if (a, b) != (0, 0)]
    barrier = pltpu.get_barrier_semaphore()
    for a, b in remote:
        if a < 1:
            with_peer(
                b,
                lambda a=a, b=b: pl.semaphore_signal(
                    barrier, inc=1, device_id=peer(a, b), device_id_type=MESH
                ),
            )

    for edge, b in ((0, -1), (lat_count - 1, 1)):

        @pl.when(lat == edge)
        def _(b=b):
            for a in (-1, 0, 1):
                slots[slot_of(a, b)] = jnp.zeros((HALF, 128), jnp.bfloat16)

    loads[1].wait()
    loads[2].wait()
    cells = cells_ref[0]
    live = lax.broadcasted_iota(jnp.int32, cells.shape, 1) < count_ref[...]
    target = jnp.where(live, cells, -1)
    onehot = jnp.where(
        lax.broadcasted_iota(jnp.int32, (CELLS, cells.shape[1]), 0) == target, 1.0, 0.0
    ).astype(jnp.bfloat16)
    for load in obs_loads:
        load.wait()
    summed = lax.dot_general(
        onehot, obs_ref[0, 0], (((1,), (1,)), ((), ())), preferred_element_type=jnp.float32
    )
    slots[CENTRE] = jnp.concatenate([summed[:HALF], summed[HALF:]], axis=1).astype(jnp.bfloat16)

    at_edge = (lat == 0) | (lat == lat_count - 1)
    pl.semaphore_wait(barrier, jnp.where(at_edge, 3, 5))
    copies = []
    for a, b in remote:
        copies.append(
            (
                a,
                b,
                pltpu.make_async_remote_copy(
                    src_ref=slots.at[CENTRE],
                    dst_ref=slots.at[slot_of(-a, -b)],
                    send_sem=send_sems.at[slot_of(a, b)],
                    recv_sem=recv_sems.at[slot_of(-a, -b)],
                    device_id=peer(a, b),
                    device_id_type=MESH,
                ),
            )
        )
    for a, b, copy in copies:
        if a >= 0:
            with_peer(b, copy.start)
    for b in (-1, 0, 1):
        with_peer(
            b,
            lambda b=b: pl.semaphore_signal(
                ready_sem, inc=1, device_id=peer(1, b), device_id_type=MESH
            ),
        )
    for load in loads[3:]:
        load.start()

    lanes = lax.broadcasted_iota(jnp.int32, (64, 128), 1)
    low_mask = jnp.where(lanes < 64, 1.0, 0.0).astype(jnp.bfloat16)
    high_mask = jnp.where(lanes < 64, 0.0, 1.0).astype(jnp.bfloat16)

    loads[3].wait()
    loads[4].wait()
    enc = enc_ref[...]
    composite(enc, near_ref, composite_ref, 3, 9, low_mask, high_mask)

    loads[5].wait()
    composite(enc, far_ref, composite_ref, 0, 3, low_mask, high_mask)
    centre = slice((CENTRE + 3) * 64, (CENTRE + 4) * 64)
    composite_ref[centre] = (
        composite_ref[centre].astype(jnp.float32) + enc.astype(jnp.float32)
    ).astype(jnp.bfloat16)

    pl.semaphore_wait(ready_sem, jnp.where(at_edge, 2, 3))
    for a, b, copy in copies:
        if a < 0:
            with_peer(b, copy.start)

    def await_from(a):
        for c, b in remote:
            if c == a:
                arrival = pltpu.make_async_remote_copy(
                    src_ref=slots.at[CENTRE],
                    dst_ref=slots.at[slot_of(a, b)],
                    send_sem=send_sems.at[slot_of(a, b)],
                    recv_sem=recv_sems.at[slot_of(a, b)],
                    device_id=peer(a, b),
                    device_id_type=MESH,
                )
                with_peer(b, arrival.wait_recv)

    half_lon = LON // 2

    def blocks_of(a):
        return [
            slots[slot_of(a, b)].astype(jnp.float32).reshape(half_lon, LAT, 128)
            for b in (-1, 0, 1)
        ]

    left = lax.broadcasted_iota(jnp.int32, (1, LAT, 128), 2) < 64

    def lat_shifted(rows_of):
        row = lax.broadcasted_iota(jnp.int32, rows_of[0].shape, 1)
        before = jnp.where(row == 0, pltpu.roll(rows_of[0], 1, 1), pltpu.roll(rows_of[1], 1, 1))
        after = jnp.where(
            row == LAT - 1,
            pltpu.roll(rows_of[2], LAT - 1, 1),
            pltpu.roll(rows_of[1], LAT - 1, 1),
        )
        return [before, rows_of[1], after]

    def stacked(taps):
        taps = [tap.reshape(HALF, 128) for tap in taps]
        left_half = lax.broadcasted_iota(jnp.int32, (HALF, 128), 1) < 64
        columns = []
        for first, second in zip(taps[::2], taps[1::2]):
            upper = jnp.where(left_half, first, pltpu.roll(second, 64, 1))
            lower = jnp.where(left_half, pltpu.roll(first, 64, 1), second)
            columns.append(jnp.concatenate([upper, lower], axis=0).astype(jnp.bfloat16))
        return jnp.concatenate(columns, axis=1)

    channels = enc.shape[1]
    late_rows = 6 * 64

    await_from(0)
    await_from(1)
    own, plus = blocks_of(0), blocks_of(1)
    ahead = [
        jnp.concatenate([own[b], pltpu.roll(jnp.where(left, plus[b][:1], own[b][:1]), 64, 2)], 0)
        for b in range(3)
    ]
    ahead = lat_shifted(ahead)
    early = stacked(
        own
        + plus
        + [piece[:half_lon] for piece in ahead]
        + [piece[1 : 1 + half_lon] for piece in ahead]
    )
    for start in range(0, channels, CHUNK):
        block = slice(start, start + CHUNK)
        total_ref[:, block] = jnp.dot(
            early, composite_ref[late_rows:, block], preferred_element_type=jnp.float32
        )

    await_from(-1)
    own, minus = blocks_of(0), blocks_of(-1)
    behind = []
    for b in range(3):
        first = jnp.where(left, own[b][half_lon - 1 :], minus[b][half_lon - 1 :])
        behind.append(jnp.concatenate([pltpu.roll(first, 64, 2), own[b][: half_lon - 1]], 0))
    late = stacked(minus + lat_shifted(behind))
    for start in range(0, channels, CHUNK):
        block = slice(start, start + CHUNK)
        total = total_ref[:, block] + jnp.dot(
            late, composite_ref[:late_rows, block], preferred_element_type=jnp.float32
        )
        total_ref[:, block] = total
        inner = 0.7978845608 * (total + 0.044715 * (total * total * total))
        activ_ref[:, block] = (0.5 * total * (1.0 + jnp.tanh(inner))).astype(jnp.bfloat16)

    loads[6].wait()
    for a, b, copy in copies:
        with_peer(b, copy.wait_send)


def on_device(
    lon_count,
    lat_count,
    obs_rows,
    obs_cells,
    obs_counts,
    enc_weight,
    near_kernel_weight,
    far_kernel_weight,
    mix_weight,
):
    channels = mix_weight.shape[0]
    operands = (
        jnp.swapaxes(obs_rows, 2, 3),
        obs_cells,
        obs_counts,
        enc_weight,
        near_kernel_weight,
        far_kernel_weight,
        mix_weight,
    )
    total, activ, mix = pl.pallas_call(
        functools.partial(kernel, lon_count, lat_count),
        out_shape=[
            jax.ShapeDtypeStruct((CELLS, channels), jnp.float32),
            jax.ShapeDtypeStruct((CELLS, channels), jnp.bfloat16),
            jax.ShapeDtypeStruct(mix_weight.shape, jnp.bfloat16),
        ],
        in_specs=[pl.BlockSpec(memory_space=pltpu.HBM)] * len(operands),
        out_specs=[pl.BlockSpec(memory_space=pltpu.VMEM)] * 3,
        scratch_shapes=[pltpu.VMEM(array.shape, array.dtype) for array in operands[:-1]]
        + [
            pltpu.VMEM((9, HALF, 128), jnp.bfloat16),
            pltpu.VMEM((18 * 64, channels), jnp.bfloat16),
            pltpu.SemaphoreType.DMA((7,)),
            pltpu.SemaphoreType.DMA((OBS_PARTS,)),
            pltpu.SemaphoreType.DMA((9,)),
            pltpu.SemaphoreType.DMA((9,)),
            pltpu.SemaphoreType.REGULAR,
        ],
        compiler_params=pltpu.CompilerParams(
            collective_id=0, has_side_effects=True, vmem_limit_bytes=24 * 1024 * 1024
        ),
    )(
        *[
            array if array is obs_counts else pltpu.with_memory_space_constraint(array, pltpu.HBM)
            for array in operands
        ]
    )
    mixed = jnp.dot(activ, mix, preferred_element_type=jnp.float32)
    return (total + mixed).astype(jnp.bfloat16).reshape(LON, LAT, channels)


def solution(mesh):
    return jax.shard_map(
        functools.partial(on_device, mesh.shape["lon"], mesh.shape["lat"]),
        mesh=mesh,
        in_specs=(
            P("lon", "lat", None, None),
            P("lon", "lat", None),
            P("lon", "lat"),
            P(),
            P(),
            P(),
            P(),
        ),
        out_specs=P("lon", "lat", None),
        check_vma=False,
    )
```

```python
import functools

import jax
import jax.numpy as jnp
from jax import lax
from jax.experimental import pallas as pl
from jax.experimental.pallas import tpu as pltpu
from jax.sharding import PartitionSpec as P

LON = 8
LAT = 8
CELLS = LON * LAT
HALF = CELLS // 2
MESH = pl.DeviceIdType.MESH
OFFSETS = [(a, b) for a in (-1, 0, 1) for b in (-1, 0, 1)]
CENTRE = 4
OBS_PARTS = 4
CHUNK = 256


def slot_of(a, b):
    return (a + 1) * 3 + (b + 1)


def composite(enc, weight_ref, composite_ref, late, early, low_mask, high_mask):
    features, channels = enc.shape
    zero = jnp.zeros((features, 128), jnp.bfloat16)

    def tap(t, carry):
        taps = weight_ref[t // 3, t % 3]
        for start in range(0, channels, CHUNK):
            left = taps[:, start : start + 128]
            right = taps[:, start + 128 : start + 256]
            blocks = jnp.concatenate(
                [
                    jnp.concatenate([left * low_mask, zero], axis=1),
                    jnp.concatenate([left * high_mask, zero], axis=1),
                    jnp.concatenate([zero, right * low_mask], axis=1),
                    jnp.concatenate([zero, right * high_mask], axis=1),
                ],
                axis=0,
            )
            product = jnp.dot(
                enc[:, start : start + CHUNK], blocks, preferred_element_type=jnp.float32
            )
            row = pl.multiple_of((t + jnp.where(t < 3, late, early)) * features, features)
            composite_ref[pl.ds(row, features), start : start + CHUNK] = product.astype(
                jnp.bfloat16
            )
        return carry

    lax.fori_loop(0, 9, tap, 0)


def kernel(
    lon_count,
    lat_count,
    obs_hbm,
    cells_hbm,
    count_hbm,
    enc_hbm,
    near_hbm,
    far_hbm,
    mix_hbm,
    out_ref,
    obs_ref,
    cells_ref,
    count_ref,
    enc_ref,
    near_ref,
    far_ref,
    mix_ref,
    total_ref,
    activ_ref,
    slots,
    composite_ref,
    local_sems,
    obs_sems,
    send_sems,
    recv_sems,
    ready_sem,
):
    pairs = [
        (obs_hbm, obs_ref),
        (cells_hbm, cells_ref),
        (count_hbm, count_ref),
        (enc_hbm, enc_ref),
        (near_hbm, near_ref),
        (far_hbm, far_ref),
        (mix_hbm, mix_ref),
    ]
    loads = [
        pltpu.make_async_copy(source, target, local_sems.at[i])
        for i, (source, target) in enumerate(pairs)
    ]
    features = obs_ref.shape[2] // OBS_PARTS
    obs_loads = []
    for i in range(OBS_PARTS):
        part = (0, 0, slice(i * features, (i + 1) * features))
        obs_loads.append(
            pltpu.make_async_copy(obs_hbm.at[part], obs_ref.at[part], obs_sems.at[i])
        )
    for load in loads[1:3] + obs_loads:
        load.start()

    lon = lax.axis_index("lon")
    lat = lax.axis_index("lat")

    def peer(a, b):
        return {"lon": lax.rem(lon + a + lon_count, lon_count), "lat": lat + b}

    def with_peer(b, body):
        if b == 0:
            body()
        elif b < 0:
            pl.when(lat > 0)(body)
        else:
            pl.when(lat < lat_count - 1)(body)

    remote = [(a, b) for a in (1, 0, -1) for b in (-1, 0, 1) if (a, b) != (0, 0)]
    barrier = pltpu.get_barrier_semaphore()
    for a, b in remote:
        if a < 1:
            with_peer(
                b,
                lambda a=a, b=b: pl.semaphore_signal(
                    barrier, inc=1, device_id=peer(a, b), device_id_type=MESH
                ),
            )

    for edge, b in ((0, -1), (lat_count - 1, 1)):

        @pl.when(lat == edge)
        def _(b=b):
            for a in (-1, 0, 1):
                slots[slot_of(a, b)] = jnp.zeros((HALF, 128), jnp.bfloat16)

    loads[1].wait()
    loads[2].wait()
    cells = cells_ref[0]
    live = lax.broadcasted_iota(jnp.int32, cells.shape, 1) < count_ref[...]
    target = jnp.where(live, cells, -1)
    onehot = jnp.where(
        lax.broadcasted_iota(jnp.int32, (CELLS, cells.shape[1]), 0) == target, 1.0, 0.0
    ).astype(jnp.bfloat16)
    for load in obs_loads:
        load.wait()
    summed = lax.dot_general(
        onehot, obs_ref[0, 0], (((1,), (1,)), ((), ())), preferred_element_type=jnp.float32
    )
    slots[CENTRE] = jnp.concatenate([summed[:HALF], summed[HALF:]], axis=1).astype(jnp.bfloat16)

    at_edge = (lat == 0) | (lat == lat_count - 1)
    pl.semaphore_wait(barrier, jnp.where(at_edge, 3, 5))
    copies = []
    for a, b in remote:
        copies.append(
            (
                a,
                b,
                pltpu.make_async_remote_copy(
                    src_ref=slots.at[CENTRE],
                    dst_ref=slots.at[slot_of(-a, -b)],
                    send_sem=send_sems.at[slot_of(a, b)],
                    recv_sem=recv_sems.at[slot_of(-a, -b)],
                    device_id=peer(a, b),
                    device_id_type=MESH,
                ),
            )
        )
    for a, b, copy in copies:
        if a >= 0:
            with_peer(b, copy.start)
    for b in (-1, 0, 1):
        with_peer(
            b,
            lambda b=b: pl.semaphore_signal(
                ready_sem, inc=1, device_id=peer(1, b), device_id_type=MESH
            ),
        )
    for load in loads[3:]:
        load.start()

    lanes = lax.broadcasted_iota(jnp.int32, (64, 128), 1)
    low_mask = jnp.where(lanes < 64, 1.0, 0.0).astype(jnp.bfloat16)
    high_mask = jnp.where(lanes < 64, 0.0, 1.0).astype(jnp.bfloat16)

    loads[3].wait()
    loads[4].wait()
    enc = enc_ref[...]
    composite(enc, near_ref, composite_ref, 3, 9, low_mask, high_mask)

    loads[5].wait()
    composite(enc, far_ref, composite_ref, 0, 3, low_mask, high_mask)
    centre = slice((CENTRE + 3) * 64, (CENTRE + 4) * 64)
    composite_ref[centre] = (
        composite_ref[centre].astype(jnp.float32) + enc.astype(jnp.float32)
    ).astype(jnp.bfloat16)

    pl.semaphore_wait(ready_sem, jnp.where(at_edge, 2, 3))
    for a, b, copy in copies:
        if a < 0:
            with_peer(b, copy.start)

    def await_from(a):
        for c, b in remote:
            if c == a:
                arrival = pltpu.make_async_remote_copy(
                    src_ref=slots.at[CENTRE],
                    dst_ref=slots.at[slot_of(a, b)],
                    send_sem=send_sems.at[slot_of(a, b)],
                    recv_sem=recv_sems.at[slot_of(a, b)],
                    device_id=peer(a, b),
                    device_id_type=MESH,
                )
                with_peer(b, arrival.wait_recv)

    half_lon = LON // 2

    def blocks_of(a):
        return [
            slots[slot_of(a, b)].astype(jnp.float32).reshape(half_lon, LAT, 128)
            for b in (-1, 0, 1)
        ]

    left = lax.broadcasted_iota(jnp.int32, (1, LAT, 128), 2) < 64

    def lat_shifted(rows_of):
        row = lax.broadcasted_iota(jnp.int32, rows_of[0].shape, 1)
        before = jnp.where(row == 0, pltpu.roll(rows_of[0], 1, 1), pltpu.roll(rows_of[1], 1, 1))
        after = jnp.where(
            row == LAT - 1,
            pltpu.roll(rows_of[2], LAT - 1, 1),
            pltpu.roll(rows_of[1], LAT - 1, 1),
        )
        return [before, rows_of[1], after]

    def stacked(taps):
        taps = [tap.reshape(HALF, 128) for tap in taps]
        left_half = lax.broadcasted_iota(jnp.int32, (HALF, 128), 1) < 64
        columns = []
        for first, second in zip(taps[::2], taps[1::2]):
            upper = jnp.where(left_half, first, pltpu.roll(second, 64, 1))
            lower = jnp.where(left_half, pltpu.roll(first, 64, 1), second)
            columns.append(jnp.concatenate([upper, lower], axis=0).astype(jnp.bfloat16))
        return jnp.concatenate(columns, axis=1)

    channels = enc.shape[1]
    late_rows = 6 * 64

    await_from(0)
    await_from(1)
    own, plus = blocks_of(0), blocks_of(1)
    ahead = [
        jnp.concatenate([own[b], pltpu.roll(jnp.where(left, plus[b][:1], own[b][:1]), 64, 2)], 0)
        for b in range(3)
    ]
    ahead = lat_shifted(ahead)
    early = stacked(
        own
        + plus
        + [piece[:half_lon] for piece in ahead]
        + [piece[1 : 1 + half_lon] for piece in ahead]
    )
    for start in range(0, channels, CHUNK):
        block = slice(start, start + CHUNK)
        total_ref[:, block] = jnp.dot(
            early, composite_ref[late_rows:, block], preferred_element_type=jnp.float32
        )

    await_from(-1)
    own, minus = blocks_of(0), blocks_of(-1)
    behind = []
    for b in range(3):
        first = jnp.where(left, own[b][half_lon - 1 :], minus[b][half_lon - 1 :])
        behind.append(jnp.concatenate([pltpu.roll(first, 64, 2), own[b][: half_lon - 1]], 0))
    late = stacked(minus + lat_shifted(behind))
    for start in range(0, channels, CHUNK):
        block = slice(start, start + CHUNK)
        total = total_ref[:, block] + jnp.dot(
            late, composite_ref[:late_rows, block], preferred_element_type=jnp.float32
        )
        total_ref[:, block] = total
        inner = 0.7978845608 * (total + 0.044715 * (total * total * total))
        activ_ref[:, block] = (0.5 * total * (1.0 + jnp.tanh(inner))).astype(jnp.bfloat16)

    loads[6].wait()
    for start in range(0, channels, CHUNK):
        block = slice(start, start + CHUNK)
        mixed = jnp.dot(activ_ref[...], mix_ref[:, block], preferred_element_type=jnp.float32)
        out_ref[:, :, block] = (
            (total_ref[:, block] + mixed).astype(jnp.bfloat16).reshape(LON, LAT, CHUNK)
        )
    for a, b, copy in copies:
        with_peer(b, copy.wait_send)


def on_device(
    lon_count,
    lat_count,
    obs_rows,
    obs_cells,
    obs_counts,
    enc_weight,
    near_kernel_weight,
    far_kernel_weight,
    mix_weight,
):
    channels = mix_weight.shape[0]
    operands = (
        jnp.swapaxes(obs_rows, 2, 3),
        obs_cells,
        obs_counts,
        enc_weight,
        near_kernel_weight,
        far_kernel_weight,
        mix_weight,
    )
    return pl.pallas_call(
        functools.partial(kernel, lon_count, lat_count),
        out_shape=jax.ShapeDtypeStruct((LON, LAT, channels), jnp.bfloat16),
        in_specs=[pl.BlockSpec(memory_space=pltpu.HBM)] * len(operands),
        out_specs=pl.BlockSpec(memory_space=pltpu.VMEM),
        scratch_shapes=[pltpu.VMEM(array.shape, array.dtype) for array in operands]
        + [
            pltpu.VMEM((CELLS, channels), jnp.float32),
            pltpu.VMEM((CELLS, channels), jnp.bfloat16),
            pltpu.VMEM((9, HALF, 128), jnp.bfloat16),
            pltpu.VMEM((18 * 64, channels), jnp.bfloat16),
            pltpu.SemaphoreType.DMA((7,)),
            pltpu.SemaphoreType.DMA((OBS_PARTS,)),
            pltpu.SemaphoreType.DMA((9,)),
            pltpu.SemaphoreType.DMA((9,)),
            pltpu.SemaphoreType.REGULAR,
        ],
        compiler_params=pltpu.CompilerParams(
            collective_id=0, has_side_effects=True, vmem_limit_bytes=24 * 1024 * 1024
        ),
    )(
        *[
            array if array is obs_counts else pltpu.with_memory_space_constraint(array, pltpu.HBM)
            for array in operands
        ]
    )


def solution(mesh):
    return jax.shard_map(
        functools.partial(on_device, mesh.shape["lon"], mesh.shape["lat"]),
        mesh=mesh,
        in_specs=(
            P("lon", "lat", None, None),
            P("lon", "lat", None),
            P("lon", "lat"),
            P(),
            P(),
            P(),
            P(),
        ),
        out_specs=P("lon", "lat", None),
        check_vma=False,
    )
```

```python
import functools

import jax
import jax.numpy as jnp
from jax import lax
from jax.experimental import pallas as pl
from jax.experimental.pallas import tpu as pltpu
from jax.sharding import PartitionSpec as P

LON = 8
LAT = 8
CELLS = LON * LAT
HALF = CELLS // 2
MESH = pl.DeviceIdType.MESH
OFFSETS = [(a, b) for a in (-1, 0, 1) for b in (-1, 0, 1)]
CENTRE = 4
OBS_PARTS = 4
CHUNK = 256


def slot_of(a, b):
    return (a + 1) * 3 + (b + 1)


def composite(enc, weight_ref, composite_ref, late, early, low_mask, high_mask):
    features, channels = enc.shape
    zero = jnp.zeros((features, 128), jnp.bfloat16)

    def tap(t, carry):
        taps = weight_ref[t // 3, t % 3]
        for start in range(0, channels, CHUNK):
            left = taps[:, start : start + 128]
            right = taps[:, start + 128 : start + 256]
            blocks = jnp.concatenate(
                [
                    jnp.concatenate([left * low_mask, zero], axis=1),
                    jnp.concatenate([left * high_mask, zero], axis=1),
                    jnp.concatenate([zero, right * low_mask], axis=1),
                    jnp.concatenate([zero, right * high_mask], axis=1),
                ],
                axis=0,
            )
            product = jnp.dot(
                enc[:, start : start + CHUNK], blocks, preferred_element_type=jnp.float32
            )
            row = pl.multiple_of((t + jnp.where(t < 3, late, early)) * features, features)
            composite_ref[pl.ds(row, features), start : start + CHUNK] = product.astype(
                jnp.bfloat16
            )
        return carry

    lax.fori_loop(0, 9, tap, 0)


def kernel(
    lon_count,
    lat_count,
    obs_hbm,
    cells_hbm,
    count_hbm,
    enc_hbm,
    near_hbm,
    far_hbm,
    mix_hbm,
    out_ref,
    obs_ref,
    cells_ref,
    count_ref,
    enc_ref,
    near_ref,
    far_ref,
    mix_ref,
    total_ref,
    slots,
    composite_ref,
    local_sems,
    obs_sems,
    send_sems,
    recv_sems,
    ready_sem,
):
    pairs = [
        (obs_hbm, obs_ref),
        (cells_hbm, cells_ref),
        (count_hbm, count_ref),
        (enc_hbm, enc_ref),
        (near_hbm, near_ref),
        (far_hbm, far_ref),
        (mix_hbm, mix_ref),
    ]
    loads = [
        pltpu.make_async_copy(source, target, local_sems.at[i])
        for i, (source, target) in enumerate(pairs)
    ]
    features = obs_ref.shape[2] // OBS_PARTS
    obs_loads = []
    for i in range(OBS_PARTS):
        part = (0, 0, slice(i * features, (i + 1) * features))
        obs_loads.append(
            pltpu.make_async_copy(obs_hbm.at[part], obs_ref.at[part], obs_sems.at[i])
        )
    for load in loads[1:3] + obs_loads:
        load.start()

    lon = lax.axis_index("lon")
    lat = lax.axis_index("lat")

    def peer(a, b):
        return {"lon": lax.rem(lon + a + lon_count, lon_count), "lat": lat + b}

    def with_peer(b, body):
        if b == 0:
            body()
        elif b < 0:
            pl.when(lat > 0)(body)
        else:
            pl.when(lat < lat_count - 1)(body)

    remote = [(a, b) for a in (1, 0, -1) for b in (-1, 0, 1) if (a, b) != (0, 0)]
    barrier = pltpu.get_barrier_semaphore()
    for a, b in remote:
        if a < 1:
            with_peer(
                b,
                lambda a=a, b=b: pl.semaphore_signal(
                    barrier, inc=1, device_id=peer(a, b), device_id_type=MESH
                ),
            )

    for edge, b in ((0, -1), (lat_count - 1, 1)):

        @pl.when(lat == edge)
        def _(b=b):
            for a in (-1, 0, 1):
                slots[slot_of(a, b)] = jnp.zeros((HALF, 128), jnp.bfloat16)

    loads[1].wait()
    loads[2].wait()
    cells = cells_ref[0]
    live = lax.broadcasted_iota(jnp.int32, cells.shape, 1) < count_ref[...]
    target = jnp.where(live, cells, -1)
    onehot = jnp.where(
        lax.broadcasted_iota(jnp.int32, (CELLS, cells.shape[1]), 0) == target, 1.0, 0.0
    ).astype(jnp.bfloat16)
    for load in obs_loads:
        load.wait()
    summed = lax.dot_general(
        onehot, obs_ref[0, 0], (((1,), (1,)), ((), ())), preferred_element_type=jnp.float32
    )
    slots[CENTRE] = jnp.concatenate([summed[:HALF], summed[HALF:]], axis=1).astype(jnp.bfloat16)

    at_edge = (lat == 0) | (lat == lat_count - 1)
    pl.semaphore_wait(barrier, jnp.where(at_edge, 3, 5))
    copies = []
    for a, b in remote:
        copies.append(
            (
                a,
                b,
                pltpu.make_async_remote_copy(
                    src_ref=slots.at[CENTRE],
                    dst_ref=slots.at[slot_of(-a, -b)],
                    send_sem=send_sems.at[slot_of(a, b)],
                    recv_sem=recv_sems.at[slot_of(-a, -b)],
                    device_id=peer(a, b),
                    device_id_type=MESH,
                ),
            )
        )
    for a, b, copy in copies:
        if a >= 0:
            with_peer(b, copy.start)
    for b in (-1, 0, 1):
        with_peer(
            b,
            lambda b=b: pl.semaphore_signal(
                ready_sem, inc=1, device_id=peer(1, b), device_id_type=MESH
            ),
        )
    for load in loads[3:]:
        load.start()

    lanes = lax.broadcasted_iota(jnp.int32, (64, 128), 1)
    low_mask = jnp.where(lanes < 64, 1.0, 0.0).astype(jnp.bfloat16)
    high_mask = jnp.where(lanes < 64, 0.0, 1.0).astype(jnp.bfloat16)

    loads[3].wait()
    loads[4].wait()
    enc = enc_ref[...]
    composite(enc, near_ref, composite_ref, 3, 9, low_mask, high_mask)

    loads[5].wait()
    composite(enc, far_ref, composite_ref, 0, 3, low_mask, high_mask)
    centre = slice((CENTRE + 3) * 64, (CENTRE + 4) * 64)
    composite_ref[centre] = (
        composite_ref[centre].astype(jnp.float32) + enc.astype(jnp.float32)
    ).astype(jnp.bfloat16)

    pl.semaphore_wait(ready_sem, jnp.where(at_edge, 2, 3))
    for a, b, copy in copies:
        if a < 0:
            with_peer(b, copy.start)

    def await_from(a):
        for c, b in remote:
            if c == a:
                arrival = pltpu.make_async_remote_copy(
                    src_ref=slots.at[CENTRE],
                    dst_ref=slots.at[slot_of(a, b)],
                    send_sem=send_sems.at[slot_of(a, b)],
                    recv_sem=recv_sems.at[slot_of(a, b)],
                    device_id=peer(a, b),
                    device_id_type=MESH,
                )
                with_peer(b, arrival.wait_recv)

    half_lon = LON // 2

    def blocks_of(a):
        return [
            slots[slot_of(a, b)].astype(jnp.float32).reshape(half_lon, LAT, 128)
            for b in (-1, 0, 1)
        ]

    left = lax.broadcasted_iota(jnp.int32, (1, LAT, 128), 2) < 64

    def lat_shifted(rows_of):
        row = lax.broadcasted_iota(jnp.int32, rows_of[0].shape, 1)
        before = jnp.where(row == 0, pltpu.roll(rows_of[0], 1, 1), pltpu.roll(rows_of[1], 1, 1))
        after = jnp.where(
            row == LAT - 1,
            pltpu.roll(rows_of[2], LAT - 1, 1),
            pltpu.roll(rows_of[1], LAT - 1, 1),
        )
        return [before, rows_of[1], after]

    def stacked(taps):
        taps = [tap.reshape(HALF, 128) for tap in taps]
        left_half = lax.broadcasted_iota(jnp.int32, (HALF, 128), 1) < 64
        columns = []
        for first, second in zip(taps[::2], taps[1::2]):
            upper = jnp.where(left_half, first, pltpu.roll(second, 64, 1))
            lower = jnp.where(left_half, pltpu.roll(first, 64, 1), second)
            columns.append(jnp.concatenate([upper, lower], axis=0).astype(jnp.bfloat16))
        return jnp.concatenate(columns, axis=1)

    channels = enc.shape[1]
    late_rows = 6 * 64

    await_from(0)
    await_from(1)
    own, plus = blocks_of(0), blocks_of(1)
    ahead = [
        jnp.concatenate([own[b], pltpu.roll(jnp.where(left, plus[b][:1], own[b][:1]), 64, 2)], 0)
        for b in range(3)
    ]
    ahead = lat_shifted(ahead)
    early = stacked(
        own
        + plus
        + [piece[:half_lon] for piece in ahead]
        + [piece[1 : 1 + half_lon] for piece in ahead]
    )
    for start in range(0, channels, CHUNK):
        block = slice(start, start + CHUNK)
        total_ref[:, block] = jnp.dot(
            early, composite_ref[late_rows:, block], preferred_element_type=jnp.float32
        )

    loads[6].wait()
    await_from(-1)
    own, minus = blocks_of(0), blocks_of(-1)
    behind = []
    for b in range(3):
        first = jnp.where(left, own[b][half_lon - 1 :], minus[b][half_lon - 1 :])
        behind.append(jnp.concatenate([pltpu.roll(first, 64, 2), own[b][: half_lon - 1]], 0))
    late = stacked(minus + lat_shifted(behind))
    activs = []
    for start in range(0, channels, CHUNK):
        block = slice(start, start + CHUNK)
        total = total_ref[:, block] + jnp.dot(
            late, composite_ref[:late_rows, block], preferred_element_type=jnp.float32
        )
        total_ref[:, block] = total
        inner = 0.7978845608 * (total + 0.044715 * (total * total * total))
        activs.append((0.5 * total * (1.0 + jnp.tanh(inner))).astype(jnp.bfloat16))

    activ = jnp.concatenate(activs, axis=1)
    for start in range(0, channels, CHUNK):
        block = slice(start, start + CHUNK)
        mixed = jnp.dot(activ, mix_ref[:, block], preferred_element_type=jnp.float32)
        out_ref[:, :, block] = (
            (total_ref[:, block] + mixed).astype(jnp.bfloat16).reshape(LON, LAT, CHUNK)
        )
    for a, b, copy in copies:
        with_peer(b, copy.wait_send)


def on_device(
    lon_count,
    lat_count,
    obs_rows,
    obs_cells,
    obs_counts,
    enc_weight,
    near_kernel_weight,
    far_kernel_weight,
    mix_weight,
):
    channels = mix_weight.shape[0]
    operands = (
        jnp.swapaxes(obs_rows, 2, 3),
        obs_cells,
        obs_counts,
        enc_weight,
        near_kernel_weight,
        far_kernel_weight,
        mix_weight,
    )
    return pl.pallas_call(
        functools.partial(kernel, lon_count, lat_count),
        out_shape=jax.ShapeDtypeStruct((LON, LAT, channels), jnp.bfloat16),
        in_specs=[pl.BlockSpec(memory_space=pltpu.HBM)] * len(operands),
        out_specs=pl.BlockSpec(memory_space=pltpu.VMEM),
        scratch_shapes=[pltpu.VMEM(array.shape, array.dtype) for array in operands]
        + [
            pltpu.VMEM((CELLS, channels), jnp.float32),
            pltpu.VMEM((9, HALF, 128), jnp.bfloat16),
            pltpu.VMEM((18 * 64, channels), jnp.bfloat16),
            pltpu.SemaphoreType.DMA((7,)),
            pltpu.SemaphoreType.DMA((OBS_PARTS,)),
            pltpu.SemaphoreType.DMA((9,)),
            pltpu.SemaphoreType.DMA((9,)),
            pltpu.SemaphoreType.REGULAR,
        ],
        compiler_params=pltpu.CompilerParams(
            collective_id=0, has_side_effects=True, vmem_limit_bytes=24 * 1024 * 1024
        ),
    )(
        *[
            array if array is obs_counts else pltpu.with_memory_space_constraint(array, pltpu.HBM)
            for array in operands
        ]
    )


def solution(mesh):
    return jax.shard_map(
        functools.partial(on_device, mesh.shape["lon"], mesh.shape["lat"]),
        mesh=mesh,
        in_specs=(
            P("lon", "lat", None, None),
            P("lon", "lat", None),
            P("lon", "lat"),
            P(),
            P(),
            P(),
            P(),
        ),
        out_specs=P("lon", "lat", None),
        check_vma=False,
    )
```

```python
import functools

import jax
import jax.numpy as jnp
from jax import lax
from jax.experimental import pallas as pl
from jax.experimental.pallas import tpu as pltpu
from jax.sharding import PartitionSpec as P

LON = 8
LAT = 8
CELLS = LON * LAT
HALF = CELLS // 2
MESH = pl.DeviceIdType.MESH
OFFSETS = [(a, b) for a in (-1, 0, 1) for b in (-1, 0, 1)]
CENTRE = 4
OBS_PARTS = 8
CHUNK = 256


def slot_of(a, b):
    return (a + 1) * 3 + (b + 1)


def composite(enc, weight_ref, composite_ref, late, early, low_mask, high_mask):
    features, channels = enc.shape
    zero = jnp.zeros((features, 128), jnp.bfloat16)

    def tap(t, carry):
        taps = weight_ref[t // 3, t % 3]
        for start in range(0, channels, CHUNK):
            left = taps[:, start : start + 128]
            right = taps[:, start + 128 : start + 256]
            blocks = jnp.concatenate(
                [
                    jnp.concatenate([left * low_mask, zero], axis=1),
                    jnp.concatenate([left * high_mask, zero], axis=1),
                    jnp.concatenate([zero, right * low_mask], axis=1),
                    jnp.concatenate([zero, right * high_mask], axis=1),
                ],
                axis=0,
            )
            product = jnp.dot(
                enc[:, start : start + CHUNK], blocks, preferred_element_type=jnp.float32
            )
            row = pl.multiple_of((t + jnp.where(t < 3, late, early)) * features, features)
            composite_ref[pl.ds(row, features), start : start + CHUNK] = product.astype(
                jnp.bfloat16
            )
        return carry

    lax.fori_loop(0, 9, tap, 0)


def kernel(
    lon_count,
    lat_count,
    obs_hbm,
    cells_hbm,
    count_hbm,
    enc_hbm,
    near_hbm,
    far_hbm,
    mix_hbm,
    out_ref,
    obs_ref,
    cells_ref,
    count_ref,
    enc_ref,
    near_ref,
    far_ref,
    mix_ref,
    total_ref,
    slots,
    composite_ref,
    local_sems,
    obs_sems,
    send_sems,
    recv_sems,
    ready_sem,
):
    pairs = [
        (obs_hbm, obs_ref),
        (cells_hbm, cells_ref),
        (count_hbm, count_ref),
        (enc_hbm, enc_ref),
        (near_hbm, near_ref),
        (far_hbm, far_ref),
        (mix_hbm, mix_ref),
    ]
    loads = [
        pltpu.make_async_copy(source, target, local_sems.at[i])
        for i, (source, target) in enumerate(pairs)
    ]
    features = obs_ref.shape[2] // OBS_PARTS
    obs_loads = []
    for i in range(OBS_PARTS):
        part = (0, 0, slice(i * features, (i + 1) * features))
        obs_loads.append(
            pltpu.make_async_copy(obs_hbm.at[part], obs_ref.at[part], obs_sems.at[i])
        )
    for load in loads[1:3] + obs_loads:
        load.start()

    lon = lax.axis_index("lon")
    lat = lax.axis_index("lat")

    def peer(a, b):
        return {"lon": lax.rem(lon + a + lon_count, lon_count), "lat": lat + b}

    def with_peer(b, body):
        if b == 0:
            body()
        elif b < 0:
            pl.when(lat > 0)(body)
        else:
            pl.when(lat < lat_count - 1)(body)

    remote = [(a, b) for a in (1, 0, -1) for b in (-1, 0, 1) if (a, b) != (0, 0)]
    barrier = pltpu.get_barrier_semaphore()
    for a, b in remote:
        if a < 1:
            with_peer(
                b,
                lambda a=a, b=b: pl.semaphore_signal(
                    barrier, inc=1, device_id=peer(a, b), device_id_type=MESH
                ),
            )

    for edge, b in ((0, -1), (lat_count - 1, 1)):

        @pl.when(lat == edge)
        def _(b=b):
            for a in (-1, 0, 1):
                slots[slot_of(a, b)] = jnp.zeros((HALF, 128), jnp.bfloat16)

    loads[1].wait()
    loads[2].wait()
    cells = cells_ref[0]
    live = lax.broadcasted_iota(jnp.int32, cells.shape, 1) < count_ref[...]
    target = jnp.where(live, cells, -1)
    onehot = jnp.where(
        lax.broadcasted_iota(jnp.int32, (CELLS, cells.shape[1]), 0) == target, 1.0, 0.0
    ).astype(jnp.bfloat16)
    for load in obs_loads:
        load.wait()
    summed = lax.dot_general(
        onehot, obs_ref[0, 0], (((1,), (1,)), ((), ())), preferred_element_type=jnp.float32
    )
    slots[CENTRE] = jnp.concatenate([summed[:HALF], summed[HALF:]], axis=1).astype(jnp.bfloat16)

    at_edge = (lat == 0) | (lat == lat_count - 1)
    pl.semaphore_wait(barrier, jnp.where(at_edge, 3, 5))
    copies = []
    for a, b in remote:
        copies.append(
            (
                a,
                b,
                pltpu.make_async_remote_copy(
                    src_ref=slots.at[CENTRE],
                    dst_ref=slots.at[slot_of(-a, -b)],
                    send_sem=send_sems.at[slot_of(a, b)],
                    recv_sem=recv_sems.at[slot_of(-a, -b)],
                    device_id=peer(a, b),
                    device_id_type=MESH,
                ),
            )
        )
    for a, b, copy in copies:
        if a >= 0:
            with_peer(b, copy.start)
    for b in (-1, 0, 1):
        with_peer(
            b,
            lambda b=b: pl.semaphore_signal(
                ready_sem, inc=1, device_id=peer(1, b), device_id_type=MESH
            ),
        )
    for load in loads[3:]:
        load.start()

    lanes = lax.broadcasted_iota(jnp.int32, (64, 128), 1)
    low_mask = jnp.where(lanes < 64, 1.0, 0.0).astype(jnp.bfloat16)
    high_mask = jnp.where(lanes < 64, 0.0, 1.0).astype(jnp.bfloat16)

    loads[3].wait()
    loads[4].wait()
    enc = enc_ref[...]
    composite(enc, near_ref, composite_ref, 3, 9, low_mask, high_mask)

    loads[5].wait()
    composite(enc, far_ref, composite_ref, 0, 3, low_mask, high_mask)
    centre = slice((CENTRE + 3) * 64, (CENTRE + 4) * 64)
    composite_ref[centre] = (
        composite_ref[centre].astype(jnp.float32) + enc.astype(jnp.float32)
    ).astype(jnp.bfloat16)

    pl.semaphore_wait(ready_sem, jnp.where(at_edge, 2, 3))
    for a, b, copy in copies:
        if a < 0:
            with_peer(b, copy.start)

    def await_from(a):
        for c, b in remote:
            if c == a:
                arrival = pltpu.make_async_remote_copy(
                    src_ref=slots.at[CENTRE],
                    dst_ref=slots.at[slot_of(a, b)],
                    send_sem=send_sems.at[slot_of(a, b)],
                    recv_sem=recv_sems.at[slot_of(a, b)],
                    device_id=peer(a, b),
                    device_id_type=MESH,
                )
                with_peer(b, arrival.wait_recv)

    half_lon = LON // 2

    def blocks_of(a):
        return [
            slots[slot_of(a, b)].astype(jnp.float32).reshape(half_lon, LAT, 128)
            for b in (-1, 0, 1)
        ]

    left = lax.broadcasted_iota(jnp.int32, (1, LAT, 128), 2) < 64

    def lat_shifted(rows_of):
        row = lax.broadcasted_iota(jnp.int32, rows_of[0].shape, 1)
        before = jnp.where(row == 0, pltpu.roll(rows_of[0], 1, 1), pltpu.roll(rows_of[1], 1, 1))
        after = jnp.where(
            row == LAT - 1,
            pltpu.roll(rows_of[2], LAT - 1, 1),
            pltpu.roll(rows_of[1], LAT - 1, 1),
        )
        return [before, rows_of[1], after]

    def stacked(taps):
        taps = [tap.reshape(HALF, 128) for tap in taps]
        left_half = lax.broadcasted_iota(jnp.int32, (HALF, 128), 1) < 64
        columns = []
        for first, second in zip(taps[::2], taps[1::2]):
            upper = jnp.where(left_half, first, pltpu.roll(second, 64, 1))
            lower = jnp.where(left_half, pltpu.roll(first, 64, 1), second)
            columns.append(jnp.concatenate([upper, lower], axis=0).astype(jnp.bfloat16))
        return jnp.concatenate(columns, axis=1)

    channels = enc.shape[1]
    late_rows = 6 * 64

    await_from(0)
    await_from(1)
    own, plus = blocks_of(0), blocks_of(1)
    ahead = [
        jnp.concatenate([own[b], pltpu.roll(jnp.where(left, plus[b][:1], own[b][:1]), 64, 2)], 0)
        for b in range(3)
    ]
    ahead = lat_shifted(ahead)
    early = stacked(
        own
        + plus
        + [piece[:half_lon] for piece in ahead]
        + [piece[1 : 1 + half_lon] for piece in ahead]
    )
    for start in range(0, channels, CHUNK):
        block = slice(start, start + CHUNK)
        total_ref[:, block] = jnp.dot(
            early, composite_ref[late_rows:, block], preferred_element_type=jnp.float32
        )

    loads[6].wait()
    await_from(-1)
    own, minus = blocks_of(0), blocks_of(-1)
    behind = []
    for b in range(3):
        first = jnp.where(left, own[b][half_lon - 1 :], minus[b][half_lon - 1 :])
        behind.append(jnp.concatenate([pltpu.roll(first, 64, 2), own[b][: half_lon - 1]], 0))
    late = stacked(minus + lat_shifted(behind))
    activs = []
    for start in range(0, channels, CHUNK):
        block = slice(start, start + CHUNK)
        total = total_ref[:, block] + jnp.dot(
            late, composite_ref[:late_rows, block], preferred_element_type=jnp.float32
        )
        total_ref[:, block] = total
        inner = 0.7978845608 * (total + 0.044715 * (total * total * total))
        activs.append((0.5 * total * (1.0 + jnp.tanh(inner))).astype(jnp.bfloat16))

    activ = jnp.concatenate(activs, axis=1)
    for start in range(0, channels, CHUNK):
        block = slice(start, start + CHUNK)
        mixed = jnp.dot(activ, mix_ref[:, block], preferred_element_type=jnp.float32)
        out_ref[:, :, block] = (
            (total_ref[:, block] + mixed).astype(jnp.bfloat16).reshape(LON, LAT, CHUNK)
        )
    for a, b, copy in copies:
        with_peer(b, copy.wait_send)


def on_device(
    lon_count,
    lat_count,
    obs_rows,
    obs_cells,
    obs_counts,
    enc_weight,
    near_kernel_weight,
    far_kernel_weight,
    mix_weight,
):
    channels = mix_weight.shape[0]
    operands = (
        jnp.swapaxes(obs_rows, 2, 3),
        obs_cells,
        obs_counts,
        enc_weight,
        near_kernel_weight,
        far_kernel_weight,
        mix_weight,
    )
    return pl.pallas_call(
        functools.partial(kernel, lon_count, lat_count),
        out_shape=jax.ShapeDtypeStruct((LON, LAT, channels), jnp.bfloat16),
        in_specs=[pl.BlockSpec(memory_space=pltpu.HBM)] * len(operands),
        out_specs=pl.BlockSpec(memory_space=pltpu.VMEM),
        scratch_shapes=[pltpu.VMEM(array.shape, array.dtype) for array in operands]
        + [
            pltpu.VMEM((CELLS, channels), jnp.float32),
            pltpu.VMEM((9, HALF, 128), jnp.bfloat16),
            pltpu.VMEM((18 * 64, channels), jnp.bfloat16),
            pltpu.SemaphoreType.DMA((7,)),
            pltpu.SemaphoreType.DMA((OBS_PARTS,)),
            pltpu.SemaphoreType.DMA((9,)),
            pltpu.SemaphoreType.DMA((9,)),
            pltpu.SemaphoreType.REGULAR,
        ],
        compiler_params=pltpu.CompilerParams(
            collective_id=0, has_side_effects=True, vmem_limit_bytes=24 * 1024 * 1024
        ),
    )(
        *[
            array if array is obs_counts else pltpu.with_memory_space_constraint(array, pltpu.HBM)
            for array in operands
        ]
    )


def solution(mesh):
    return jax.shard_map(
        functools.partial(on_device, mesh.shape["lon"], mesh.shape["lat"]),
        mesh=mesh,
        in_specs=(
            P("lon", "lat", None, None),
            P("lon", "lat", None),
            P("lon", "lat"),
            P(),
            P(),
            P(),
            P(),
        ),
        out_specs=P("lon", "lat", None),
        check_vma=False,
    )
```
